256 devices in a mesh: genome: 32 (over z, x), anc: 4 (over y_lo, core), trait: 2 (over y_hi).
Axes of the slice: x: 4, y: 4 (y_hi: 2, y_lo: 2; y = y_hi * 2 + y_lo), z: 8, core: 2. Of those that a mesh axis runs over, the one named last changes fastest.
Arguments:
- coefficients: float32 [4, 128, 65536], P('anc', 'trait', 'genome'), may hold values from -3 to 3
- sumstats: float32 [4, 128, 65536], P('anc', 'trait', 'genome'), may hold values from -12 to 12
- linkage: bfloat16 [4, 65536, 4096], P('anc', 'genome'), may hold values from -0.09375 to 0.09375
- band_start: int32 [4, 256], P('anc', 'genome'), may hold values from 0 to 61440, as said below
- group_ids: int32 [4, 65536], P('anc', 'genome'), may hold values from 0 to 63, never falling along the last dimension, each value on 1 to 8192 neighbouring positions
- group_weight: float32 [4, 64], P('anc'), may hold values from 0.1 to 1.5
- dosage: bfloat16 [4, 2048, 65536], P('anc', None, 'genome'), may hold values from 0 to 2
Outputs:
- updated: float32 [4, 128, 65536], P('anc', 'trait', 'genome')
- scores: float32 [4, 128, 2048], P('anc', 'trait', 'genome')
The draws below stay inside these ranges and needn't reach their ends.
Inputs may be any that keep to these rules, and one draw needn't show every extreme that they name: band_start[a, u] is the first of the 4096 consecutive SNP columns stored in linkage[a] for row block u, the SNPs u * 256 to u * 256 + 255; these columns always include the block's own SNPs. `group_ids`: group ids never fall along the SNPs of an ancestry, so each group is one run of consecutive SNPs.
All inputs are finite; a program needn't handle non-finite values.
Results may differ from the reference program's by a relative error of at most 0.003.
Values may be sent and summed in bfloat16 or wider, within the bound.
No kernel may reach another device: no remote copies, remote signals or barrier semaphores. Data moves between devices by JAX's collectives and lax.ppermute only.
A program may use at most 128 MiB of HBM per device.

```python
import math
import jax
import jax.numpy as jnp
import numpy as np
from jax import lax

TRAITS = 128
ANC = 4
W = 4096
TILE = 256
M_DEV = 2048
PERSONS = 2048
SNPS = 65536
GROUPS = 64


def draw_band_start(key, part):
    block_count = SNPS // TILE
    spare = W - TILE
    anchors = jnp.arange(block_count, dtype=jnp.int32) * TILE
    jitter = jax.random.randint(key, (ANC, block_count), 0, spare + 1, dtype=jnp.int32)
    raw_start = anchors[None, :] - jitter
    return jnp.minimum(jnp.maximum(raw_start, 0), SNPS - W).astype(jnp.int32)


def draw_sumstats(key, part):
    block_count = SNPS // TILE
    key_noise = jax.random.fold_in(key, 11)
    key_scale = jax.random.fold_in(key, 23)
    noise = jnp.clip(jax.random.normal(key_noise, (ANC, TRAITS, SNPS), jnp.float32), -4.0, 4.0)
    block_scale = jnp.exp(jax.random.uniform(key_scale, (ANC, 1, block_count), jnp.float32, -0.69, 0.69))
    block_scale = jnp.repeat(block_scale, TILE, axis=2)
    trend = 3.0 ** (jnp.arange(SNPS, dtype=jnp.float32) / SNPS)
    return (0.5 * noise * block_scale * trend[None, None, :]).astype(jnp.float32)


def levels(key, shape, shards, smallest, largest):
    def one(axis_at, blocks):
        draws = jax.random.uniform(jax.random.fold_in(jax.random.fold_in(key, 6), axis_at), (blocks,), jnp.float32, smallest / len(shards), largest / len(shards))
        return jnp.repeat(jnp.exp(draws), shape[axis_at] // blocks).reshape((-1,) + (1,) * (len(shape) - axis_at - 1))

    level = one(*shards[0])
    for cut in shards[1:]:
        level = level * one(*cut)
    return level


def length_profile(number_of, total, most, lean):
    weights = [(1 << 20) // math.isqrt(rank ** lean) + 1 for rank in range(2, number_of + 1)]
    surplus, given = total - most - (number_of - 1), [1] * (number_of - 1)
    while surplus > 0:
        movable = [i for i in range(number_of - 1) if given[i] < most]
        mass, budget = sum([weights[i] for i in movable]), surplus
        for i in movable:
            extra = min(most - given[i], max(1, budget * weights[i] // mass), surplus)
            given[i] = given[i] + extra
            surplus = surplus - extra
    return np.array([most] + given)


def ragged_sizes(rng, count, total, bound, lean):
    if count == 2:
        one = jax.random.randint(rng, (), max(1, total - bound), min(bound, total - 1) + 1)
        return jnp.stack([one, total - one])
    tallies = jnp.asarray(length_profile(count, total, bound, lean), jnp.int32)
    couples = (count - 1) // 2
    source_of, taker = tallies[1:1 + 2 * couples:2], tallies[2:2 + 2 * couples:2]
    margin = jnp.minimum(source_of - 1, bound - taker)
    shifted = jax.random.randint(jax.random.fold_in(rng, 1), (couples,), 0, 1 << 20) % (margin + 1)
    tallies = tallies.at[1:1 + 2 * couples:2].set(source_of - shifted).at[2:2 + 2 * couples:2].set(taker + shifted)
    return tallies[jax.random.permutation(jax.random.fold_in(rng, 2), count)]


def gaussian(key, shape, scale, most, split=(), kind=jnp.bfloat16):
    entries = jax.random.normal(key, shape, jnp.float32) * scale
    if len(split) > 0:
        entries = levels(key, shape, split, -0.22, 0.18) * entries
    return jnp.clip(entries, min=-most, max=most).astype(kind)


def setup_inputs(seed: int = 0) -> dict:
    splits = jax.random.split(jax.random.key(seed), 8)
    coefficients = gaussian(splits[0], (ANC, TRAITS, SNPS), 0.5, 3.0, ((0, 4), (1, 2), (2, 32)), jnp.float32)
    sumstats = draw_sumstats(jax.random.fold_in(splits[7], 71), 0)
    linkage = gaussian(splits[2], (ANC, SNPS, W), W ** -0.5, 0.09375, ((0, 4), (1, 32)))
    band_start = draw_band_start(jax.random.fold_in(splits[7], 71), 0)
    group_ids = jax.vmap(lambda own: jnp.searchsorted(jnp.cumsum(ragged_sizes(own, GROUPS, SNPS, 4 * M_DEV, 2)), jnp.arange(SNPS), side="right"))(jax.random.split(splits[4], ANC)).reshape((ANC, SNPS)).astype(jnp.int32)
    group_weight = jnp.clip(jnp.exp(math.log(1.5) - 2.7080502 * jax.random.uniform(splits[5], (ANC, GROUPS), jnp.float32) ** levels(splits[5], (ANC, GROUPS), ((0, 4),), -0.2, 0.2)), 0.1, 1.5)
    dosage = jnp.clip(2.0 * jax.random.uniform(splits[6], (ANC, PERSONS, SNPS), jnp.float32) ** levels(splits[6], (ANC, PERSONS, SNPS), ((0, 4), (2, 32)), -0.2, 0.2), 0.0, 2.0).astype(jnp.bfloat16)
    return dict(coefficients=coefficients, sumstats=sumstats, linkage=linkage, band_start=band_start, group_ids=group_ids, group_weight=group_weight, dosage=dosage)


step_size = 0.5
merging = 0.5
epsilon = 1e-06

def band_apply(low_copy, band, starts):
    padded = jnp.pad(low_copy.astype(jnp.float32), ((0, 0), (W, W)))
    band_tiles = band.reshape(SNPS // TILE, TILE, W)

    def per_tile(tile_item):
        block_rows, begin_at = tile_item
        window = lax.dynamic_slice_in_dim(padded, (begin_at + W).astype(jnp.int32), W, 1)
        return jnp.dot(window, block_rows.astype(jnp.float32).T, precision=lax.Precision.HIGHEST)
    products = lax.map(per_tile, (band_tiles, starts))
    return jnp.transpose(products, (1, 0, 2)).reshape(TRAITS, SNPS)

def reference(coefficients, sumstats, linkage, band_start, group_ids, group_weight, dosage):
    mean_coef = lax.optimization_barrier(jnp.sum(coefficients, axis=0)) / ANC
    update_list = []
    score_list = []
    for ancestry in range(ANC):
        current = coefficients[ancestry]
        band_product = band_apply(current.astype(jnp.bfloat16), linkage[ancestry], band_start[ancestry])
        gradient = current + band_product - sumstats[ancestry] + merging * (current - mean_coef)
        proposal = current - step_size * gradient
        trait_total = lax.optimization_barrier(jnp.sum(proposal * proposal, axis=0))
        group_list = group_ids[ancestry]
        squares = jax.ops.segment_sum(trait_total, group_list, num_segments=GROUPS)
        counts = jax.ops.segment_sum(jnp.ones_like(trait_total), group_list, num_segments=GROUPS)
        threshold = step_size * group_weight[ancestry] * jnp.sqrt(counts * TRAITS)
        factor = jnp.maximum(0.0, 1.0 - threshold / jnp.sqrt(squares + epsilon))
        updated = proposal * factor[group_list][None, :]
        genotype = dosage[ancestry]
        scores = jnp.dot(updated.astype(jnp.bfloat16), genotype.T, preferred_element_type=jnp.float32) / math.sqrt(SNPS)
        update_list.append(updated)
        score_list.append(scores)
    return (jnp.stack(update_list), jnp.stack(score_list))
```

```python
import functools
import math

import jax
import jax.numpy as jnp
from jax import lax
from jax.experimental import pallas as pl
from jax.experimental.pallas import tpu as pltpu
from jax.sharding import PartitionSpec as P

TILE = 256
LANES = 128
GROUPS = 64

step_size = 0.5
merging = 0.5
epsilon = 1e-06

NT = (((1,), (1,)), ((), ()))


def band_kernel(
    ancestries, starts, far_below, below, own, above, far_above, band, coef, targets, anc1, anc2, anc3, ids,
    proposal, sums, extended, square_acc, count_acc,
):
    unit = pl.program_id(0)
    rows, snps = own.shape
    width = band.shape[1]

    @pl.when(unit == 0)
    def _():
        for at, piece in enumerate((far_below, below, own, above, far_above)):
            extended[:, at * snps : (at + 1) * snps] = piece[...].astype(jnp.float32)
        extended[:, 5 * snps :] = jnp.zeros((rows, LANES), jnp.float32)
        square_acc[...] = jnp.zeros_like(square_acc)
        count_acc[...] = jnp.zeros_like(count_acc)

    start = starts[unit]
    base = pl.multiple_of((start // LANES) * LANES, LANES)
    shift = start - base
    back = lax.rem(LANES - shift, LANES)
    lane = lax.broadcasted_iota(jnp.int32, (rows, LANES), 1)
    keep = lane < LANES - shift
    window = []
    turned = pltpu.roll(extended[:, pl.ds(base, LANES)], back, 1)
    for at in range(width // LANES):
        following = pltpu.roll(extended[:, pl.ds(base + (at + 1) * LANES, LANES)], back, 1)
        window.append(jnp.where(keep, turned, following).astype(jnp.bfloat16))
        turned = following
    window = jnp.concatenate(window, axis=1)
    product = lax.dot_general(window, band[...], NT, preferred_element_type=jnp.float32)

    current = coef[...]
    total = current + anc1[...].astype(jnp.float32) + anc2[...].astype(jnp.float32) + anc3[...].astype(jnp.float32)
    gradient = current + product - targets[...] + merging * (current - total * (1.0 / ancestries))
    value = current - step_size * gradient
    proposal[...] = value
    part = jnp.sum(value * value, axis=0, keepdims=True)
    group = lax.broadcasted_iota(jnp.int32, (GROUPS, LANES), 0)
    squares = square_acc[...]
    counts = count_acc[...]
    for at in range(TILE // LANES):
        here = ids[:, at * LANES : (at + 1) * LANES] == group
        squares += jnp.where(here, part[:, at * LANES : (at + 1) * LANES], 0.0)
        counts += jnp.where(here, 1.0, 0.0)
    square_acc[...] = squares
    count_acc[...] = counts

    @pl.when(unit == pl.num_programs(0) - 1)
    def _():
        place = lax.broadcasted_iota(jnp.int32, (GROUPS, LANES), 1)
        square_col = jnp.sum(squares, axis=1, keepdims=True)
        count_col = jnp.sum(counts, axis=1, keepdims=True)
        both = jnp.where(place == group, square_col, 0.0) + jnp.where(place == group + GROUPS, count_col * rows, 0.0)
        sums[...] = jnp.broadcast_to(jnp.sum(both, axis=0, keepdims=True), sums.shape)


def band_step(starts, pieces, band, coef, targets, ancs, ids, peers, ancestries):
    rows, snps = coef.shape
    width = band.shape[1]
    whole = pl.BlockSpec((rows, snps), lambda u: (0, 0))
    tile = pl.BlockSpec((rows, TILE), lambda u: (0, u))
    return pl.pallas_call(
        functools.partial(band_kernel, ancestries),
        grid=(snps // TILE,),
        in_specs=[pl.BlockSpec(memory_space=pltpu.SMEM)]
        + [whole] * 5
        + [pl.BlockSpec((TILE, width), lambda u: (u, 0)), tile, tile, tile, tile, tile,
           pl.BlockSpec((1, TILE), lambda u: (0, u))],
        out_specs=[tile, pl.BlockSpec((peers, LANES), lambda u: (0, 0))],
        out_shape=[
            jax.ShapeDtypeStruct((rows, snps), jnp.float32),
            jax.ShapeDtypeStruct((peers, LANES), jnp.float32),
        ],
        scratch_shapes=[
            pltpu.VMEM((rows, 5 * snps + LANES), jnp.float32),
            pltpu.VMEM((GROUPS, LANES), jnp.float32),
            pltpu.VMEM((GROUPS, LANES), jnp.float32),
        ],
        compiler_params=pltpu.CompilerParams(
            dimension_semantics=("arbitrary",), vmem_limit_bytes=52 << 20
        ),
        cost_estimate=pl.CostEstimate(
            flops=2 * rows * snps * width, bytes_accessed=2 * snps * width + 24 * rows * snps, transcendentals=0
        ),
        name="band_step",
    )(starts, *pieces, band, coef, targets, *ancs, ids)


def score_kernel(scale, sums, weights, ids, proposal, dosage, updated, partial, low):
    rows, snps = proposal.shape

    @pl.when(pl.program_id(0) == 0)
    def _():
        total = jnp.sum(sums[...], axis=0, keepdims=True)
        spread = jnp.broadcast_to(total, (GROUPS, LANES))
        group = lax.broadcasted_iota(jnp.int32, (GROUPS, LANES), 0)
        place = lax.broadcasted_iota(jnp.int32, (GROUPS, LANES), 1)
        squares = jnp.sum(jnp.where(place == group, spread, 0.0), axis=1, keepdims=True)
        counts = jnp.sum(jnp.where(place == group + GROUPS, spread, 0.0), axis=1, keepdims=True)
        weight_row = jnp.broadcast_to(weights[...], (GROUPS, GROUPS))
        here = lax.broadcasted_iota(jnp.int32, (GROUPS, GROUPS), 0) == lax.broadcasted_iota(
            jnp.int32, (GROUPS, GROUPS), 1
        )
        weight = jnp.sum(jnp.where(here, weight_row, 0.0), axis=1, keepdims=True)
        threshold = step_size * weight * jnp.sqrt(counts)
        factor = jnp.maximum(0.0, 1.0 - threshold / jnp.sqrt(squares + epsilon))
        factor = jnp.broadcast_to(factor, (GROUPS, LANES))
        for at in range(snps // LANES):
            cut = slice(at * LANES, (at + 1) * LANES)
            chosen = jnp.sum(jnp.where(ids[:, cut] == group, factor, 0.0), axis=0, keepdims=True)
            value = proposal[:, cut] * chosen
            updated[:, cut] = value
            low[:, cut] = value.astype(jnp.bfloat16)

    product = lax.dot_general(low[...], dosage[...], NT, preferred_element_type=jnp.float32) * scale
    half = rows // 2
    left = lax.broadcasted_iota(jnp.int32, (half, LANES), 1) < LANES // 2
    for at in range(product.shape[1] // LANES):
        cut = product[:, at * LANES : (at + 1) * LANES]
        first, second = cut[:half], cut[half:]
        partial[2 * at] = jnp.where(left, first, pltpu.roll(second, LANES // 2, 1)).astype(partial.dtype)
        partial[2 * at + 1] = jnp.where(left, pltpu.roll(first, LANES // 2, 1), second).astype(partial.dtype)


def score_step(sums, weights, ids, proposal, dosage, genome_count):
    rows, snps = proposal.shape
    persons = dosage.shape[0]
    block = 256
    each = persons // genome_count
    whole = pl.BlockSpec((rows, snps), lambda p: (0, 0))
    return pl.pallas_call(
        functools.partial(score_kernel, 1.0 / math.sqrt(snps * genome_count)),
        grid=(persons // block,),
        in_specs=[
            pl.BlockSpec(sums.shape, lambda p: (0, 0)),
            pl.BlockSpec((1, GROUPS), lambda p: (0, 0)),
            pl.BlockSpec((1, snps), lambda p: (0, 0)),
            whole,
            pl.BlockSpec((block, snps), lambda p: (p, 0)),
        ],
        out_specs=[whole, pl.BlockSpec((block // each, rows // 2, LANES), lambda p: (p, 0, 0))],
        out_shape=[
            jax.ShapeDtypeStruct((rows, snps), jnp.float32),
            jax.ShapeDtypeStruct((genome_count, rows // 2, LANES), jnp.bfloat16),
        ],
        scratch_shapes=[pltpu.VMEM((rows, snps), jnp.bfloat16)],
        compiler_params=pltpu.CompilerParams(
            dimension_semantics=("arbitrary",), vmem_limit_bytes=32 << 20
        ),
        cost_estimate=pl.CostEstimate(
            flops=2 * rows * snps * persons, bytes_accessed=2 * snps * persons + 8 * rows * snps, transcendentals=0
        ),
        name="score_step",
    )(sums, weights, ids, proposal, dosage)


def total_kernel(arrived, scores):
    total = jnp.sum(arrived[...].astype(jnp.float32), axis=0)
    half = LANES // 2
    rows = total.shape[0]
    scores[:rows] = total[:, :half]
    scores[rows:] = pltpu.roll(total, half, 1)[:, :half]


def total_step(arrived):
    rows = 2 * arrived.shape[1]
    return pl.pallas_call(
        total_kernel,
        out_shape=jax.ShapeDtypeStruct((rows, LANES // 2), jnp.float32),
        name="total_step",
    )(arrived)


def passed_along(block, axis, distance):
    devices = range(lax.axis_size(axis))
    route = [(i - distance, i) for i in devices if i - distance in devices]
    return lax.ppermute(block, axis, route)


def per_device(coefficients, sumstats, linkage, band_start, group_ids, group_weight, dosage):
    current = coefficients[0]
    targets = sumstats[0]
    band = linkage[0]
    starts = band_start[0]
    snp_rows = current.shape[1]
    genome_count = lax.axis_size("genome")
    anc_count = lax.axis_size("anc")
    position = lax.axis_index("genome")
    low_copy = current.astype(jnp.bfloat16)
    pieces = [
        passed_along(low_copy, "genome", 2),
        passed_along(low_copy, "genome", 1),
        low_copy,
        passed_along(low_copy, "genome", -1),
        passed_along(low_copy, "genome", -2),
    ]
    ancs = [
        lax.ppermute(low_copy, "anc", [(i, i ^ k) for i in range(anc_count)]) for k in range(1, anc_count)
    ]
    local_start = starts - position * snp_rows + 2 * snp_rows
    peers = genome_count * lax.axis_size("trait")
    proposal, sums = band_step(
        local_start, pieces, band, current, targets, ancs, group_ids, peers, anc_count
    )
    arrived = lax.all_to_all(
        sums.reshape(peers, 1, LANES), ("genome", "trait"), split_axis=0, concat_axis=0, tiled=True
    ).reshape(peers, LANES)
    updated, partial = score_step(arrived, group_weight, group_ids, proposal, dosage[0], genome_count)
    received = lax.all_to_all(partial, "genome", split_axis=0, concat_axis=0, tiled=True)
    scores = total_step(received)
    return (updated[None], scores[None])


def solution(mesh):
    in_specs = (
        P("anc", "trait", "genome"),
        P("anc", "trait", "genome"),
        P("anc", "genome", None),
        P("anc", "genome"),
        P("anc", "genome"),
        P("anc", None),
        P("anc", None, "genome"),
    )
    out_specs = (P("anc", "trait", "genome"), P("anc", "trait", "genome"))
    return jax.shard_map(
        per_device, mesh=mesh, in_specs=in_specs, out_specs=out_specs, check_vma=False
    )
```

```python
import functools
import math

import jax
import jax.numpy as jnp
from jax import lax
from jax.experimental import pallas as pl
from jax.experimental.pallas import tpu as pltpu
from jax.sharding import PartitionSpec as P

TILE = 256
LANES = 128
GROUPS = 64

step_size = 0.5
merging = 0.5
epsilon = 1e-06

NT = (((1,), (1,)), ((), ()))


def place_of():
    return lax.axis_index("genome")


def cast_kernel(coef, low, first, second):
    skip = jnp.where(lax.rem(place_of(), 4) < 2, TILE, 0)
    low[...] = coef[...].astype(jnp.bfloat16)
    for begin, out in ((skip, first), (TILE - skip, second)):
        out[...] = coef[:, pl.ds(pl.multiple_of(begin, TILE), out.shape[1])].astype(jnp.bfloat16)


def cast_step(coef):
    rows, snps = coef.shape
    part = jax.ShapeDtypeStruct((rows, snps - TILE), jnp.bfloat16)
    vmem = pl.BlockSpec(memory_space=pltpu.VMEM)
    return pl.pallas_call(
        cast_kernel,
        in_specs=[vmem],
        out_specs=[vmem] * 3,
        out_shape=[jax.ShapeDtypeStruct((rows, snps), jnp.bfloat16), part, part],
        name="cast_step",
    )(coef)


def window_tiles(source, base, shift, count):
    rows = source.shape[0]
    back = lax.rem(LANES - shift, LANES)
    keep = lax.broadcasted_iota(jnp.int32, (rows, LANES), 1) < LANES - shift
    tiles = []
    turned = pltpu.roll(source[:, pl.ds(base, LANES)], back, 1)
    for at in range(count):
        following = pltpu.roll(source[:, pl.ds(base + (at + 1) * LANES, LANES)], back, 1)
        tiles.append(jnp.where(keep, turned, following).astype(jnp.bfloat16))
        turned = following
    return jnp.concatenate(tiles, axis=1)


def near_kernel(starts, own, first, second, band, product, held, extended, sems):
    rows, snps = own.shape
    place = place_of()
    above_first = lax.rem(place, 2) == 0
    first_at = jnp.where(above_first, 3 * snps, snps)
    width = band.shape[1]
    units = snps // TILE

    depth = 3

    def copy_of(unit):
        cut = pl.ds(pl.multiple_of(unit * TILE, TILE), TILE)
        return pltpu.make_async_copy(band.at[cut], held.at[cut], sems.at[unit])

    for unit in range(depth):
        copy_of(unit).start()
    extended[:, :snps] = jnp.zeros((rows, snps), jnp.float32)
    extended[:, 2 * snps : 3 * snps] = own[...].astype(jnp.float32)
    extended[:, 4 * snps :] = jnp.zeros((rows, snps + LANES), jnp.float32)
    for at, piece in ((first_at, first), (4 * snps - first_at, second)):
        extended[:, pl.ds(pl.multiple_of(at, LANES), snps)] = piece[...].astype(jnp.float32)

    def per_unit(unit, carry):
        start = starts[unit] + (2 - place) * snps
        base = pl.multiple_of((start // LANES) * LANES, LANES)
        window = window_tiles(extended, base, start - base, width // LANES)
        copy_of(unit).wait()

        @pl.when(unit + depth < units)
        def _():
            copy_of(unit + depth).start()

        cut = pl.ds(pl.multiple_of(unit * TILE, TILE), TILE)
        product[:, cut] = lax.dot_general(window, held[cut, :], NT, preferred_element_type=jnp.float32)
        return carry

    lax.fori_loop(0, units, per_unit, 0)


def near_step(starts, own, first, second, band):
    rows, snps = own.shape
    width = band.shape[1]
    smem = pl.BlockSpec(memory_space=pltpu.SMEM)
    vmem = pl.BlockSpec(memory_space=pltpu.VMEM)
    return pl.pallas_call(
        near_kernel,
        in_specs=[smem, vmem, vmem, vmem, pl.BlockSpec(memory_space=pltpu.HBM)],
        out_specs=[vmem, vmem],
        out_shape=[
            jax.ShapeDtypeStruct((rows, snps), jnp.float32),
            jax.ShapeDtypeStruct(band.shape, band.dtype),
        ],
        scratch_shapes=[
            pltpu.VMEM((rows, 5 * snps + LANES), jnp.float32),
            pltpu.SemaphoreType.DMA((snps // TILE,)),
        ],
        compiler_params=pltpu.CompilerParams(vmem_limit_bytes=10 << 20),
        cost_estimate=pl.CostEstimate(
            flops=2 * rows * snps * width, bytes_accessed=2 * snps * width + 8 * rows * snps, transcendentals=0
        ),
        name="near_step",
    )(starts, own, first, second, pltpu.with_memory_space_constraint(band, pltpu.HBM))


def far_kernel(
    ancestries, starts, first, second, held, product, coef, targets, core_copy, pair_copy, ids,
    proposal, sums, far, square_acc, count_acc,
):
    rows, snps = coef.shape
    units = snps // TILE
    reach = 2 * TILE
    place = place_of()
    high_at = snps + 4 * TILE
    first_at = jnp.where(lax.rem(place, 4) < 2, high_at, TILE)
    far[:, snps - TILE :] = jnp.zeros((rows, far.shape[1] - snps + TILE), jnp.float32)
    for at, piece in ((first_at, first), (high_at + TILE - first_at, second)):
        far[:, pl.ds(pl.multiple_of(at, LANES), piece.shape[1])] = piece[...].astype(jnp.float32)
    square_acc[...] = jnp.zeros_like(square_acc)
    count_acc[...] = jnp.zeros_like(count_acc)
    group = lax.broadcasted_iota(jnp.int32, (GROUPS, LANES), 0)

    def per_unit(unit, carry):
        rows_from = pl.multiple_of(unit * TILE, TILE)
        cut = pl.ds(rows_from, TILE)
        start = starts[unit] + (2 - place) * snps
        tiles = held.shape[1] // TILE
        low_count = (jnp.maximum(snps - start, 0) + reach - 1) // reach
        high_count = (jnp.maximum(start - 2 * snps, 0) + reach - 1) // reach
        from_tile = jnp.where(high_count > 0, tiles - 2 * high_count, 0)
        moved = start + jnp.where(high_count > 0, high_at - 4 * snps, 0)

        def per_tile(step, total):
            column = pl.multiple_of((from_tile + 2 * step) * TILE, TILE)
            begin = moved + column
            base = pl.multiple_of((begin // LANES) * LANES, LANES)
            window = window_tiles(far, base, begin - base, reach // LANES)
            return total + lax.dot_general(
                window, held[cut, pl.ds(column, reach)], NT, preferred_element_type=jnp.float32
            )

        bands = lax.fori_loop(0, low_count + high_count, per_tile, product[:, cut])
        current = coef[:, cut]
        total = current + core_copy[:, cut].astype(jnp.float32) + pair_copy[:, cut].astype(jnp.float32)
        gradient = current + bands - targets[:, cut] + merging * (current - total * (1.0 / ancestries))
        value = current - step_size * gradient
        proposal[:, cut] = value
        part = jnp.sum(value * value, axis=0, keepdims=True)
        ids_here = ids[:, cut]
        squares = square_acc[...]
        counts = count_acc[...]
        for at in range(TILE // LANES):
            here = ids_here[:, at * LANES : (at + 1) * LANES] == group
            squares += jnp.where(here, part[:, at * LANES : (at + 1) * LANES], 0.0)
            counts += jnp.where(here, 1.0, 0.0)
        square_acc[...] = squares
        count_acc[...] = counts
        return carry

    lax.fori_loop(0, units, per_unit, 0)
    lane = lax.broadcasted_iota(jnp.int32, (GROUPS, LANES), 1)
    square_col = jnp.sum(square_acc[...], axis=1, keepdims=True)
    count_col = jnp.sum(count_acc[...], axis=1, keepdims=True)
    both = jnp.where(lane == group, square_col, 0.0) + jnp.where(lane == group + GROUPS, count_col * rows, 0.0)
    sums[...] = jnp.broadcast_to(jnp.sum(both, axis=0, keepdims=True), sums.shape)


def far_step(starts, first, second, held, product, coef, targets, core_copy, pair_copy, ids, peers, ancestries):
    rows, snps = coef.shape
    smem = pl.BlockSpec(memory_space=pltpu.SMEM)
    vmem = pl.BlockSpec(memory_space=pltpu.VMEM)
    return pl.pallas_call(
        functools.partial(far_kernel, ancestries),
        in_specs=[smem] + [vmem] * 9,
        out_specs=[vmem, vmem],
        out_shape=[
            jax.ShapeDtypeStruct((rows, snps), jnp.float32),
            jax.ShapeDtypeStruct((peers, LANES), jnp.float32),
        ],
        scratch_shapes=[
            pltpu.VMEM((rows, 2 * snps + 4 * TILE + LANES), jnp.float32),
            pltpu.VMEM((GROUPS, LANES), jnp.float32),
            pltpu.VMEM((GROUPS, LANES), jnp.float32),
        ],
        compiler_params=pltpu.CompilerParams(vmem_limit_bytes=10 << 20),
        cost_estimate=pl.CostEstimate(
            flops=2 * rows * snps * 1024, bytes_accessed=20 * rows * snps, transcendentals=0
        ),
        name="far_step",
    )(starts, first, second, held, product, coef, targets, core_copy, pair_copy, ids)


def score_kernel(scale, sums, weights, ids, proposal, dosage, updated, partial, low):
    rows, snps = proposal.shape

    @pl.when(pl.program_id(0) == 0)
    def _():
        total = jnp.sum(sums[...], axis=0, keepdims=True)
        spread = jnp.broadcast_to(total, (GROUPS, LANES))
        group = lax.broadcasted_iota(jnp.int32, (GROUPS, LANES), 0)
        place = lax.broadcasted_iota(jnp.int32, (GROUPS, LANES), 1)
        squares = jnp.sum(jnp.where(place == group, spread, 0.0), axis=1, keepdims=True)
        counts = jnp.sum(jnp.where(place == group + GROUPS, spread, 0.0), axis=1, keepdims=True)
        weight_row = jnp.broadcast_to(weights[...], (GROUPS, GROUPS))
        here = lax.broadcasted_iota(jnp.int32, (GROUPS, GROUPS), 0) == lax.broadcasted_iota(
            jnp.int32, (GROUPS, GROUPS), 1
        )
        weight = jnp.sum(jnp.where(here, weight_row, 0.0), axis=1, keepdims=True)
        threshold = step_size * weight * jnp.sqrt(counts)
        factor = jnp.maximum(0.0, 1.0 - threshold / jnp.sqrt(squares + epsilon))
        factor = jnp.broadcast_to(factor, (GROUPS, LANES))
        for at in range(snps // LANES):
            cut = slice(at * LANES, (at + 1) * LANES)
            chosen = jnp.sum(jnp.where(ids[:, cut] == group, factor, 0.0), axis=0, keepdims=True)
            value = proposal[:, cut] * chosen
            updated[:, cut] = value
            low[:, cut] = value.astype(jnp.bfloat16)

    product = lax.dot_general(low[...], dosage[...], NT, preferred_element_type=jnp.float32) * scale
    half = rows // 2
    left = lax.broadcasted_iota(jnp.int32, (half, LANES), 1) < LANES // 2
    for at in range(product.shape[1] // LANES):
        cut = product[:, at * LANES : (at + 1) * LANES]
        first, second = cut[:half], cut[half:]
        partial[2 * at] = jnp.where(left, first, pltpu.roll(second, LANES // 2, 1)).astype(partial.dtype)
        partial[2 * at + 1] = jnp.where(left, pltpu.roll(first, LANES // 2, 1), second).astype(partial.dtype)


def score_step(sums, weights, ids, proposal, dosage, genome_count):
    rows, snps = proposal.shape
    persons = dosage.shape[0]
    block = 256
    each = persons // genome_count
    whole = pl.BlockSpec((rows, snps), lambda p: (0, 0))
    return pl.pallas_call(
        functools.partial(score_kernel, 1.0 / math.sqrt(snps * genome_count)),
        grid=(persons // block,),
        in_specs=[
            pl.BlockSpec(sums.shape, lambda p: (0, 0)),
            pl.BlockSpec((1, GROUPS), lambda p: (0, 0)),
            pl.BlockSpec((1, snps), lambda p: (0, 0)),
            whole,
            pl.BlockSpec((block, snps), lambda p: (p, 0)),
        ],
        out_specs=[whole, pl.BlockSpec((block // each, rows // 2, LANES), lambda p: (p, 0, 0))],
        out_shape=[
            jax.ShapeDtypeStruct((rows, snps), jnp.float32),
            jax.ShapeDtypeStruct((genome_count, rows // 2, LANES), jnp.bfloat16),
        ],
        scratch_shapes=[pltpu.VMEM((rows, snps), jnp.bfloat16)],
        compiler_params=pltpu.CompilerParams(
            dimension_semantics=("arbitrary",), vmem_limit_bytes=32 << 20
        ),
        cost_estimate=pl.CostEstimate(
            flops=2 * rows * snps * persons, bytes_accessed=2 * snps * persons + 8 * rows * snps, transcendentals=0
        ),
        name="score_step",
    )(sums, weights, ids, proposal, dosage)


def total_kernel(arrived, scores):
    total = jnp.sum(arrived[...].astype(jnp.float32), axis=0)
    half = LANES // 2
    rows = total.shape[0]
    scores[:rows] = total[:, :half]
    scores[rows:] = pltpu.roll(total, half, 1)[:, :half]


def total_step(arrived):
    rows = 2 * arrived.shape[1]
    return pl.pallas_call(
        total_kernel,
        out_shape=jax.ShapeDtypeStruct((rows, LANES // 2), jnp.float32),
        name="total_step",
    )(arrived)


def swapped(block, axis, distance, lower):
    count = lax.axis_size(axis)
    pairs = [(i, i + distance) for i in range(count - distance) if lower(i)]
    return lax.ppermute(block, axis, pairs + [(j, i) for i, j in pairs])


def per_device(coefficients, sumstats, linkage, band_start, group_ids, group_weight, dosage):
    current = coefficients[0]
    targets = sumstats[0]
    band = linkage[0]
    starts = band_start[0]
    genome_count = lax.axis_size("genome")
    anc_count = lax.axis_size("anc")
    low_copy, send_inside, send_across = cast_step(current)
    far_inside = swapped(send_inside, "genome", 2, lambda i: i % 4 < 2)
    far_across = swapped(send_across, "genome", 2, lambda i: i % 4 >= 2)
    near_even = swapped(low_copy, "genome", 1, lambda i: i % 2 == 0)
    near_odd = swapped(low_copy, "genome", 1, lambda i: i % 2 == 1)
    core_copy = swapped(low_copy, "anc", 1, lambda i: i % 2 == 0)
    pair_sum = (current + core_copy.astype(jnp.float32)).astype(jnp.bfloat16)
    pair_copy = swapped(pair_sum, "anc", 2, lambda i: i < 2)
    product, held = near_step(starts, low_copy, near_even, near_odd, band)
    peers = genome_count * lax.axis_size("trait")
    proposal, sums = far_step(
        starts, far_inside, far_across, held, product, current, targets, core_copy, pair_copy,
        group_ids, peers, anc_count,
    )
    arrived = lax.all_to_all(
        sums.reshape(peers, 1, LANES), ("genome", "trait"), split_axis=0, concat_axis=0, tiled=True
    ).reshape(peers, LANES)
    updated, partial = score_step(arrived, group_weight, group_ids, proposal, dosage[0], genome_count)
    received = lax.all_to_all(partial, "genome", split_axis=0, concat_axis=0, tiled=True)
    scores = total_step(received)
    return (updated[None], scores[None])


def solution(mesh):
    in_specs = (
        P("anc", "trait", "genome"),
        P("anc", "trait", "genome"),
        P("anc", "genome", None),
        P("anc", "genome"),
        P("anc", "genome"),
        P("anc", None),
        P("anc", None, "genome"),
    )
    out_specs = (P("anc", "trait", "genome"), P("anc", "trait", "genome"))
    return jax.shard_map(
        per_device, mesh=mesh, in_specs=in_specs, out_specs=out_specs, check_vma=False
    )
```

```python
import functools
import math

import jax
import jax.numpy as jnp
from jax import lax
from jax.experimental import pallas as pl
from jax.experimental.pallas import tpu as pltpu
from jax.sharding import PartitionSpec as P

TILE = 256
LANES = 128
GROUPS = 64

step_size = 0.5
merging = 0.5
epsilon = 1e-06

NT = (((1,), (1,)), ((), ()))


def place_of():
    return lax.axis_index("genome")


def window_tiles(source, base, shift, count):
    rows = source.shape[0]
    back = lax.rem(LANES - shift, LANES)
    keep = lax.broadcasted_iota(jnp.int32, (rows, LANES), 1) < LANES - shift
    tiles = []
    turned = pltpu.roll(source[:, pl.ds(base, LANES)], back, 1)
    for at in range(count):
        following = pltpu.roll(source[:, pl.ds(base + (at + 1) * LANES, LANES)], back, 1)
        tiles.append(jnp.where(keep, turned, following).astype(jnp.bfloat16))
        turned = following
    return jnp.concatenate(tiles, axis=1)


def near_kernel(starts_in, own, first, second, band, product, held, extended, starts, sems, start_sem):
    rows, snps = own.shape
    place = place_of()
    above_first = lax.rem(place, 2) == 0
    first_at = jnp.where(above_first, 3 * snps, snps)
    width = band.shape[1]
    units = snps // TILE

    depth = 3

    def copy_of(unit):
        cut = pl.ds(pl.multiple_of(unit * TILE, TILE), TILE)
        return pltpu.make_async_copy(band.at[cut], held.at[cut], sems.at[unit])

    start_copy = pltpu.make_async_copy(starts_in, starts, start_sem)
    start_copy.start()
    for unit in range(depth):
        copy_of(unit).start()
    extended[:, :snps] = jnp.zeros((rows, snps), jnp.float32)
    extended[:, 2 * snps : 3 * snps] = own[...].astype(jnp.float32)
    extended[:, 4 * snps :] = jnp.zeros((rows, snps + LANES), jnp.float32)
    for at, piece in ((first_at, first), (4 * snps - first_at, second)):
        extended[:, pl.ds(pl.multiple_of(at, LANES), snps)] = piece[...].astype(jnp.float32)
    start_copy.wait()

    def per_unit(unit, carry):
        start = starts[0, unit] + (2 - place) * snps
        base = pl.multiple_of((start // LANES) * LANES, LANES)
        window = window_tiles(extended, base, start - base, width // LANES)
        copy_of(unit).wait()

        @pl.when(unit + depth < units)
        def _():
            copy_of(unit + depth).start()

        cut = pl.ds(pl.multiple_of(unit * TILE, TILE), TILE)
        product[:, cut] = lax.dot_general(window, held[cut, :], NT, preferred_element_type=jnp.float32)
        return carry

    lax.fori_loop(0, units, per_unit, 0)


def near_step(starts, own, first, second, band):
    rows, snps = own.shape
    width = band.shape[1]
    hbm = pl.BlockSpec(memory_space=pltpu.HBM)
    vmem = pl.BlockSpec(memory_space=pltpu.VMEM)
    return pl.pallas_call(
        near_kernel,
        in_specs=[hbm, vmem, vmem, vmem, hbm],
        out_specs=[vmem, vmem],
        out_shape=[
            jax.ShapeDtypeStruct((rows, snps), jnp.float32),
            jax.ShapeDtypeStruct(band.shape, band.dtype),
        ],
        scratch_shapes=[
            pltpu.VMEM((rows, 5 * snps + LANES), jnp.float32),
            pltpu.SMEM((1, snps // TILE), jnp.int32),
            pltpu.SemaphoreType.DMA((snps // TILE,)),
            pltpu.SemaphoreType.DMA,
        ],
        compiler_params=pltpu.CompilerParams(vmem_limit_bytes=10 << 20),
        cost_estimate=pl.CostEstimate(
            flops=2 * rows * snps * width, bytes_accessed=2 * snps * width + 8 * rows * snps, transcendentals=0
        ),
        name="near_step",
    )(
        pltpu.with_memory_space_constraint(starts, pltpu.HBM), own, first, second,
        pltpu.with_memory_space_constraint(band, pltpu.HBM),
    )


def far_kernel(
    ancestries, starts_in, first, second, held, product, coef, targets, core_copy, pair_copy, ids,
    proposal, sums, far, square_acc, count_acc, starts, start_sem,
):
    rows, snps = coef.shape
    units = snps // TILE
    reach = 2 * TILE
    place = place_of()
    high_at = snps + 4 * TILE
    first_at = jnp.where(lax.rem(place, 2) == 0, high_at, 0)
    start_copy = pltpu.make_async_copy(starts_in, starts, start_sem)
    start_copy.start()
    far[:, snps:high_at] = jnp.zeros((rows, high_at - snps), jnp.float32)
    far[:, high_at + snps :] = jnp.zeros((rows, LANES), jnp.float32)
    for at, piece in ((first_at, first), (high_at - first_at, second)):
        far[:, pl.ds(pl.multiple_of(at, LANES), piece.shape[1])] = piece[...].astype(jnp.float32)
    square_acc[...] = jnp.zeros_like(square_acc)
    count_acc[...] = jnp.zeros_like(count_acc)
    start_copy.wait()
    group = lax.broadcasted_iota(jnp.int32, (GROUPS, LANES), 0)

    def per_unit(unit, carry):
        rows_from = pl.multiple_of(unit * TILE, TILE)
        cut = pl.ds(rows_from, TILE)
        start = starts[0, unit] + (2 - place) * snps
        tiles = held.shape[1] // TILE
        low_count = (jnp.maximum(snps - start, 0) + reach - 1) // reach
        high_count = (jnp.maximum(start - 2 * snps, 0) + reach - 1) // reach
        from_tile = jnp.where(high_count > 0, tiles - 2 * high_count, 0)
        moved = start + jnp.where(high_count > 0, high_at - 4 * snps, 0)

        def per_tile(step, total):
            column = pl.multiple_of((from_tile + 2 * step) * TILE, TILE)
            begin = moved + column
            base = pl.multiple_of((begin // LANES) * LANES, LANES)
            window = window_tiles(far, base, begin - base, reach // LANES)
            return total + lax.dot_general(
                window, held[cut, pl.ds(column, reach)], NT, preferred_element_type=jnp.float32
            )

        bands = lax.fori_loop(0, low_count + high_count, per_tile, product[:, cut])
        current = coef[:, cut]
        total = current + core_copy[:, cut].astype(jnp.float32) + pair_copy[:, cut].astype(jnp.float32)
        gradient = current + bands - targets[:, cut] + merging * (current - total * (1.0 / ancestries))
        value = current - step_size * gradient
        proposal[:, cut] = value
        part = jnp.sum(value * value, axis=0, keepdims=True)
        ids_here = ids[:, cut]
        squares = square_acc[...]
        counts = count_acc[...]
        for at in range(TILE // LANES):
            here = ids_here[:, at * LANES : (at + 1) * LANES] == group
            squares += jnp.where(here, part[:, at * LANES : (at + 1) * LANES], 0.0)
            counts += jnp.where(here, 1.0, 0.0)
        square_acc[...] = squares
        count_acc[...] = counts
        return carry

    lax.fori_loop(0, units, per_unit, 0)
    lane = lax.broadcasted_iota(jnp.int32, (GROUPS, LANES), 1)
    square_col = jnp.sum(square_acc[...], axis=1, keepdims=True)
    count_col = jnp.sum(count_acc[...], axis=1, keepdims=True)
    both = jnp.where(lane == group, square_col, 0.0) + jnp.where(lane == group + GROUPS, count_col * rows, 0.0)
    sums[...] = jnp.broadcast_to(jnp.sum(both, axis=0, keepdims=True), sums.shape)


def far_step(starts, first, second, held, product, coef, targets, core_copy, pair_copy, ids, peers, ancestries):
    rows, snps = coef.shape
    hbm = pl.BlockSpec(memory_space=pltpu.HBM)
    vmem = pl.BlockSpec(memory_space=pltpu.VMEM)
    return pl.pallas_call(
        functools.partial(far_kernel, ancestries),
        in_specs=[hbm] + [vmem] * 9,
        out_specs=[vmem, vmem],
        out_shape=[
            jax.ShapeDtypeStruct((rows, snps), jnp.float32),
            jax.ShapeDtypeStruct((peers, LANES), jnp.float32),
        ],
        scratch_shapes=[
            pltpu.VMEM((rows, 2 * snps + 4 * TILE + LANES), jnp.float32),
            pltpu.VMEM((GROUPS, LANES), jnp.float32),
            pltpu.VMEM((GROUPS, LANES), jnp.float32),
            pltpu.SMEM((1, snps // TILE), jnp.int32),
            pltpu.SemaphoreType.DMA,
        ],
        compiler_params=pltpu.CompilerParams(vmem_limit_bytes=10 << 20),
        cost_estimate=pl.CostEstimate(
            flops=2 * rows * snps * 1024, bytes_accessed=20 * rows * snps, transcendentals=0
        ),
        name="far_step",
    )(
        pltpu.with_memory_space_constraint(starts, pltpu.HBM), first, second, held, product, coef, targets, core_copy, pair_copy, ids,
    )


def score_kernel(scale, sums, weights, ids, proposal, dosage, updated, partial, low):
    rows, snps = proposal.shape

    @pl.when(pl.program_id(0) == 0)
    def _():
        total = jnp.sum(sums[...], axis=0, keepdims=True)
        spread = jnp.broadcast_to(total, (GROUPS, LANES))
        group = lax.broadcasted_iota(jnp.int32, (GROUPS, LANES), 0)
        place = lax.broadcasted_iota(jnp.int32, (GROUPS, LANES), 1)
        squares = jnp.sum(jnp.where(place == group, spread, 0.0), axis=1, keepdims=True)
        counts = jnp.sum(jnp.where(place == group + GROUPS, spread, 0.0), axis=1, keepdims=True)
        weight_row = jnp.broadcast_to(weights[...], (GROUPS, GROUPS))
        here = lax.broadcasted_iota(jnp.int32, (GROUPS, GROUPS), 0) == lax.broadcasted_iota(
            jnp.int32, (GROUPS, GROUPS), 1
        )
        weight = jnp.sum(jnp.where(here, weight_row, 0.0), axis=1, keepdims=True)
        threshold = step_size * weight * jnp.sqrt(counts)
        factor = jnp.maximum(0.0, 1.0 - threshold / jnp.sqrt(squares + epsilon))
        factor = jnp.broadcast_to(factor, (GROUPS, LANES))
        for at in range(snps // LANES):
            cut = slice(at * LANES, (at + 1) * LANES)
            chosen = jnp.sum(jnp.where(ids[:, cut] == group, factor, 0.0), axis=0, keepdims=True)
            value = proposal[:, cut] * chosen
            updated[:, cut] = value
            low[:, cut] = value.astype(jnp.bfloat16)

    product = lax.dot_general(low[...], dosage[...], NT, preferred_element_type=jnp.float32) * scale
    half = rows // 2
    left = lax.broadcasted_iota(jnp.int32, (half, LANES), 1) < LANES // 2
    for at in range(product.shape[1] // LANES):
        cut = product[:, at * LANES : (at + 1) * LANES]
        first, second = cut[:half], cut[half:]
        partial[2 * at] = jnp.where(left, first, pltpu.roll(second, LANES // 2, 1)).astype(partial.dtype)
        partial[2 * at + 1] = jnp.where(left, pltpu.roll(first, LANES // 2, 1), second).astype(partial.dtype)


def score_step(sums, weights, ids, proposal, dosage, genome_count):
    rows, snps = proposal.shape
    persons = dosage.shape[0]
    block = 256
    each = persons // genome_count
    whole = pl.BlockSpec((rows, snps), lambda p: (0, 0))
    return pl.pallas_call(
        functools.partial(score_kernel, 1.0 / math.sqrt(snps * genome_count)),
        grid=(persons // block,),
        in_specs=[
            pl.BlockSpec(sums.shape, lambda p: (0, 0)),
            pl.BlockSpec((1, GROUPS), lambda p: (0, 0)),
            pl.BlockSpec((1, snps), lambda p: (0, 0)),
            whole,
            pl.BlockSpec((block, snps), lambda p: (p, 0)),
        ],
        out_specs=[whole, pl.BlockSpec((block // each, rows // 2, LANES), lambda p: (p, 0, 0))],
        out_shape=[
            jax.ShapeDtypeStruct((rows, snps), jnp.float32),
            jax.ShapeDtypeStruct((genome_count, rows // 2, LANES), jnp.bfloat16),
        ],
        scratch_shapes=[pltpu.VMEM((rows, snps), jnp.bfloat16)],
        compiler_params=pltpu.CompilerParams(
            dimension_semantics=("arbitrary",), vmem_limit_bytes=32 << 20
        ),
        cost_estimate=pl.CostEstimate(
            flops=2 * rows * snps * persons, bytes_accessed=2 * snps * persons + 8 * rows * snps, transcendentals=0
        ),
        name="score_step",
    )(sums, weights, ids, proposal, dosage)


def total_kernel(arrived, scores):
    total = jnp.sum(arrived[...].astype(jnp.float32), axis=0)
    half = LANES // 2
    rows = total.shape[0]
    scores[:rows] = total[:, :half]
    scores[rows:] = pltpu.roll(total, half, 1)[:, :half]


def total_step(arrived):
    rows = 2 * arrived.shape[1]
    return pl.pallas_call(
        total_kernel,
        out_shape=jax.ShapeDtypeStruct((rows, LANES // 2), jnp.float32),
        name="total_step",
    )(arrived)


def swapped(block, axis, distance, lower):
    count = lax.axis_size(axis)
    pairs = [(i, i + distance) for i in range(count - distance) if lower(i)]
    return lax.ppermute(block, axis, pairs + [(j, i) for i, j in pairs])


def per_device(coefficients, sumstats, linkage, band_start, group_ids, group_weight, dosage):
    current = coefficients[0]
    targets = sumstats[0]
    band = linkage[0]
    genome_count = lax.axis_size("genome")
    anc_count = lax.axis_size("anc")
    low_copy = current.astype(jnp.bfloat16)
    near_even = swapped(low_copy, "genome", 1, lambda i: i % 2 == 0)
    near_odd = swapped(low_copy, "genome", 1, lambda i: i % 2 == 1)
    far_even = swapped(near_odd, "genome", 1, lambda i: i % 2 == 0)
    far_odd = swapped(near_even, "genome", 1, lambda i: i % 2 == 1)
    core_copy = swapped(low_copy, "anc", 1, lambda i: i % 2 == 0)
    pair_sum = (current + core_copy.astype(jnp.float32)).astype(jnp.bfloat16)
    pair_copy = swapped(pair_sum, "anc", 2, lambda i: i < 2)
    product, held = near_step(band_start, low_copy, near_even, near_odd, band)
    peers = genome_count * lax.axis_size("trait")
    proposal, sums = far_step(
        band_start, far_even, far_odd, held, product, current, targets, core_copy, pair_copy,
        group_ids, peers, anc_count,
    )
    arrived = lax.all_to_all(
        sums.reshape(peers, 1, LANES), ("genome", "trait"), split_axis=0, concat_axis=0, tiled=True
    ).reshape(peers, LANES)
    updated, partial = score_step(arrived, group_weight, group_ids, proposal, dosage[0], genome_count)
    received = lax.all_to_all(partial, "genome", split_axis=0, concat_axis=0, tiled=True)
    scores = total_step(received)
    return (updated[None], scores[None])


def solution(mesh):
    in_specs = (
        P("anc", "trait", "genome"),
        P("anc", "trait", "genome"),
        P("anc", "genome", None),
        P("anc", "genome"),
        P("anc", "genome"),
        P("anc", None),
        P("anc", None, "genome"),
    )
    out_specs = (P("anc", "trait", "genome"), P("anc", "trait", "genome"))
    return jax.shard_map(
        per_device, mesh=mesh, in_specs=in_specs, out_specs=out_specs, check_vma=False
    )
```

```python
import functools
import math

import jax
import jax.numpy as jnp
from jax import lax
from jax.experimental import pallas as pl
from jax.experimental.pallas import tpu as pltpu
from jax.sharding import PartitionSpec as P

TILE = 256
LANES = 128
GROUPS = 64
EARLY = 4

step_size = 0.5
merging = 0.5
epsilon = 1e-06

NT = (((1,), (1,)), ((), ()))


def place_of():
    return lax.axis_index("genome")


def window_tiles(source, base, shift, count):
    rows = source.shape[0]
    back = lax.rem(LANES - shift, LANES)
    keep = lax.broadcasted_iota(jnp.int32, (rows, LANES), 1) < LANES - shift
    tiles = []
    turned = pltpu.roll(source[:, pl.ds(base, LANES)], back, 1)
    for at in range(count):
        following = pltpu.roll(source[:, pl.ds(base + (at + 1) * LANES, LANES)], back, 1)
        tiles.append(jnp.where(keep, turned, following).astype(jnp.bfloat16))
        turned = following
    return jnp.concatenate(tiles, axis=1)


def unit_copy(band, held, sems, unit, first):
    here = pl.ds(pl.multiple_of((unit - first) * TILE, TILE), TILE)
    there = pl.ds(pl.multiple_of(unit * TILE, TILE), TILE)
    return pltpu.make_async_copy(band.at[there], held.at[here], sems.at[unit - first])


def own_kernel(starts_in, own, band, product, held, padded, starts, sems, start_sem):
    rows, snps = own.shape
    units = held.shape[0] // TILE
    count = snps // TILE + 1
    depth = min(3, units)
    start_copy = pltpu.make_async_copy(starts_in, starts, start_sem)
    start_copy.start()
    for unit in range(depth):
        unit_copy(band, held, sems, unit, 0).start()
    place = place_of()
    padded[:, :snps] = jnp.zeros((rows, snps), jnp.float32)
    padded[:, snps : 2 * snps] = own[...].astype(jnp.float32)
    padded[:, 2 * snps :] = jnp.zeros((rows, padded.shape[1] - 2 * snps), jnp.float32)
    start_copy.wait()

    def per_unit(unit, carry):
        start = starts[0, unit] + (2 - place) * snps
        first_tile = jnp.clip((2 * snps - start) // TILE, 0, snps // TILE - 1)
        column = pl.multiple_of(first_tile * TILE, TILE)
        begin = start + column - snps
        base = pl.multiple_of((begin // LANES) * LANES, LANES)
        window = window_tiles(padded, base, begin - base, count * TILE // LANES)
        cut = pl.ds(pl.multiple_of(unit * TILE, TILE), TILE)
        unit_copy(band, held, sems, unit, 0).wait()

        @pl.when(unit + depth < units)
        def _():
            unit_copy(band, held, sems, unit + depth, 0).start()

        product[:, cut] = lax.dot_general(
            window, held[cut, pl.ds(column, count * TILE)], NT, preferred_element_type=jnp.float32
        )
        return carry

    lax.fori_loop(0, units, per_unit, 0)


def own_step(starts, own, band, units):
    rows, snps = own.shape
    width = band.shape[1]
    hbm = pl.BlockSpec(memory_space=pltpu.HBM)
    vmem = pl.BlockSpec(memory_space=pltpu.VMEM)
    return pl.pallas_call(
        own_kernel,
        in_specs=[hbm, vmem, hbm],
        out_specs=[vmem, vmem],
        out_shape=[
            jax.ShapeDtypeStruct((rows, units * TILE), jnp.float32),
            jax.ShapeDtypeStruct((units * TILE, width), band.dtype),
        ],
        scratch_shapes=[
            pltpu.VMEM((rows, 3 * snps + TILE + LANES), jnp.float32),
            pltpu.SMEM((1, snps // TILE), jnp.int32),
            pltpu.SemaphoreType.DMA((units,)),
            pltpu.SemaphoreType.DMA,
        ],
        compiler_params=pltpu.CompilerParams(vmem_limit_bytes=10 << 20),
        cost_estimate=pl.CostEstimate(
            flops=2 * rows * units * TILE * (snps + TILE), bytes_accessed=2 * units * TILE * width, transcendentals=0
        ),
        name="own_step",
    )(pltpu.with_memory_space_constraint(starts, pltpu.HBM), own, pltpu.with_memory_space_constraint(band, pltpu.HBM))


def near_kernel(
    starts_in, own, first, second, early, before, band, product, late, extended, starts, sems, start_sem
):
    rows, snps = first.shape
    width = band.shape[1]
    units = snps // TILE
    early_units = early.shape[0] // TILE
    count = units + 1
    start_copy = pltpu.make_async_copy(starts_in, starts, start_sem)
    start_copy.start()
    for unit in range(early_units, units):
        unit_copy(band, late, sems, unit, early_units).start()
    place = place_of()
    first_at = jnp.where(lax.rem(place, 2) == 0, 3 * snps, snps)
    for at in (0, 2, 4):
        extended[:, at * snps : (at + 1) * snps] = jnp.zeros((rows, snps), jnp.float32)
    extended[:, 5 * snps :] = jnp.zeros((rows, LANES), jnp.float32)
    for at, piece in ((first_at, first), (4 * snps - first_at, second)):
        extended[:, pl.ds(pl.multiple_of(at, LANES), snps)] = piece[...].astype(jnp.float32)
    start_copy.wait()

    def early_unit(unit, carry):
        start = starts[0, unit] + (2 - place) * snps
        cut = pl.ds(pl.multiple_of(unit * TILE, TILE), TILE)
        left = (2 * snps - start) // TILE
        skip = jnp.where(
            start > 2 * snps, (3 * snps - start) // TILE, jnp.where(start <= snps, (snps - start) // TILE, 0)
        )
        skip = jnp.clip(skip, 0, count - 2)
        both = (start > snps) & (start <= 2 * snps)
        total = before[:, cut]
        for step in range(count):
            tile = step + jnp.where(both & (step > left), count - 2, skip)
            column = pl.multiple_of(tile * TILE, TILE)
            begin = start + column
            base = pl.multiple_of((begin // LANES) * LANES, LANES)
            window = window_tiles(extended, base, begin - base, TILE // LANES)
            total += lax.dot_general(window, early[cut, pl.ds(column, TILE)], NT, preferred_element_type=jnp.float32)
        product[:, cut] = total
        return carry

    lax.fori_loop(0, early_units, early_unit, 0)
    extended[:, 2 * snps : 3 * snps] = own[...].astype(jnp.float32)

    def late_unit(unit, carry):
        start = starts[0, unit] + (2 - place) * snps
        base = pl.multiple_of((start // LANES) * LANES, LANES)
        window = window_tiles(extended, base, start - base, width // LANES)
        unit_copy(band, late, sems, unit, early_units).wait()
        here = pl.ds(pl.multiple_of((unit - early_units) * TILE, TILE), TILE)
        cut = pl.ds(pl.multiple_of(unit * TILE, TILE), TILE)
        product[:, cut] = lax.dot_general(window, late[here, :], NT, preferred_element_type=jnp.float32)
        return carry

    lax.fori_loop(early_units, units, late_unit, 0)


def near_step(starts, own, first, second, early, before, band):
    rows, snps = first.shape
    width = band.shape[1]
    late_rows = snps - early.shape[0]
    hbm = pl.BlockSpec(memory_space=pltpu.HBM)
    vmem = pl.BlockSpec(memory_space=pltpu.VMEM)
    return pl.pallas_call(
        near_kernel,
        in_specs=[hbm] + [vmem] * 5 + [hbm],
        out_specs=[vmem, vmem],
        out_shape=[
            jax.ShapeDtypeStruct((rows, snps), jnp.float32),
            jax.ShapeDtypeStruct((late_rows, width), band.dtype),
        ],
        scratch_shapes=[
            pltpu.VMEM((rows, 5 * snps + LANES), jnp.float32),
            pltpu.SMEM((1, snps // TILE), jnp.int32),
            pltpu.SemaphoreType.DMA((late_rows // TILE,)),
            pltpu.SemaphoreType.DMA,
        ],
        compiler_params=pltpu.CompilerParams(vmem_limit_bytes=10 << 20),
        cost_estimate=pl.CostEstimate(
            flops=2 * rows * snps * width, bytes_accessed=2 * late_rows * width + 8 * rows * snps, transcendentals=0
        ),
        name="near_step",
    )(
        pltpu.with_memory_space_constraint(starts, pltpu.HBM), own, first, second, early, before,
        pltpu.with_memory_space_constraint(band, pltpu.HBM),
    )


def far_kernel(
    ancestries, starts_in, first, second, early, late, product, coef, targets, core_copy, pair_copy, ids,
    proposal, sums, far, square_acc, count_acc, starts, start_sem,
):
    rows, snps = coef.shape
    units = snps // TILE
    reach = 2 * TILE
    place = place_of()
    high_at = snps + 4 * TILE
    first_at = jnp.where(lax.rem(place, 2) == 0, high_at, 0)
    start_copy = pltpu.make_async_copy(starts_in, starts, start_sem)
    start_copy.start()
    far[:, snps:high_at] = jnp.zeros((rows, high_at - snps), jnp.float32)
    far[:, high_at + snps :] = jnp.zeros((rows, LANES), jnp.float32)
    for at, piece in ((first_at, first), (high_at - first_at, second)):
        far[:, pl.ds(pl.multiple_of(at, LANES), piece.shape[1])] = piece[...].astype(jnp.float32)
    square_acc[...] = jnp.zeros_like(square_acc)
    count_acc[...] = jnp.zeros_like(count_acc)
    start_copy.wait()
    group = lax.broadcasted_iota(jnp.int32, (GROUPS, LANES), 0)

    def per_unit(held, first_unit, unit, carry):
        cut = pl.ds(pl.multiple_of(unit * TILE, TILE), TILE)
        here = pl.ds(pl.multiple_of((unit - first_unit) * TILE, TILE), TILE)
        start = starts[0, unit] + (2 - place) * snps
        tiles = held.shape[1] // TILE
        low_count = (jnp.maximum(snps - start, 0) + reach - 1) // reach
        high_count = (jnp.maximum(start - 2 * snps, 0) + reach - 1) // reach
        from_tile = jnp.where(high_count > 0, tiles - 2 * high_count, 0)
        moved = start + jnp.where(high_count > 0, high_at - 4 * snps, 0)

        def per_tile(step, total):
            column = pl.multiple_of((from_tile + 2 * step) * TILE, TILE)
            begin = moved + column
            base = pl.multiple_of((begin // LANES) * LANES, LANES)
            window = window_tiles(far, base, begin - base, reach // LANES)
            return total + lax.dot_general(
                window, held[here, pl.ds(column, reach)], NT, preferred_element_type=jnp.float32
            )

        bands = lax.fori_loop(0, low_count + high_count, per_tile, product[:, cut])
        current = coef[:, cut]
        total = current + core_copy[:, cut].astype(jnp.float32) + pair_copy[:, cut].astype(jnp.float32)
        gradient = current + bands - targets[:, cut] + merging * (current - total * (1.0 / ancestries))
        value = current - step_size * gradient
        proposal[:, cut] = value
        part = jnp.sum(value * value, axis=0, keepdims=True)
        ids_here = ids[:, cut]
        squares = square_acc[...]
        counts = count_acc[...]
        for at in range(TILE // LANES):
            here = ids_here[:, at * LANES : (at + 1) * LANES] == group
            squares += jnp.where(here, part[:, at * LANES : (at + 1) * LANES], 0.0)
            counts += jnp.where(here, 1.0, 0.0)
        square_acc[...] = squares
        count_acc[...] = counts
        return carry

    early_units = early.shape[0] // TILE
    lax.fori_loop(0, early_units, functools.partial(per_unit, early, 0), 0)
    lax.fori_loop(early_units, units, functools.partial(per_unit, late, early_units), 0)
    lane = lax.broadcasted_iota(jnp.int32, (GROUPS, LANES), 1)
    square_col = jnp.sum(square_acc[...], axis=1, keepdims=True)
    count_col = jnp.sum(count_acc[...], axis=1, keepdims=True)
    both = jnp.where(lane == group, square_col, 0.0) + jnp.where(lane == group + GROUPS, count_col * rows, 0.0)
    sums[...] = jnp.broadcast_to(jnp.sum(both, axis=0, keepdims=True), sums.shape)


def far_step(starts, first, second, early, late, product, coef, targets, core_copy, pair_copy, ids, peers, ancestries):
    rows, snps = coef.shape
    hbm = pl.BlockSpec(memory_space=pltpu.HBM)
    vmem = pl.BlockSpec(memory_space=pltpu.VMEM)
    return pl.pallas_call(
        functools.partial(far_kernel, ancestries),
        in_specs=[hbm] + [vmem] * 10,
        out_specs=[vmem, vmem],
        out_shape=[
            jax.ShapeDtypeStruct((rows, snps), jnp.float32),
            jax.ShapeDtypeStruct((peers, LANES), jnp.float32),
        ],
        scratch_shapes=[
            pltpu.VMEM((rows, 2 * snps + 4 * TILE + LANES), jnp.float32),
            pltpu.VMEM((GROUPS, LANES), jnp.float32),
            pltpu.VMEM((GROUPS, LANES), jnp.float32),
            pltpu.SMEM((1, snps // TILE), jnp.int32),
            pltpu.SemaphoreType.DMA,
        ],
        compiler_params=pltpu.CompilerParams(vmem_limit_bytes=10 << 20),
        cost_estimate=pl.CostEstimate(
            flops=2 * rows * snps * 1024, bytes_accessed=20 * rows * snps, transcendentals=0
        ),
        name="far_step",
    )(
        pltpu.with_memory_space_constraint(starts, pltpu.HBM), first, second, early, late, product, coef, targets, core_copy, pair_copy, ids,
    )


def score_kernel(scale, sums, weights, ids, proposal, dosage, updated_out, partial, low, updated, out_sem):
    rows, snps = proposal.shape
    block = TILE
    total = jnp.sum(sums[...], axis=0, keepdims=True)
    spread = jnp.broadcast_to(total, (GROUPS, LANES))
    group = lax.broadcasted_iota(jnp.int32, (GROUPS, LANES), 0)
    place = lax.broadcasted_iota(jnp.int32, (GROUPS, LANES), 1)
    squares = jnp.sum(jnp.where(place == group, spread, 0.0), axis=1, keepdims=True)
    counts = jnp.sum(jnp.where(place == group + GROUPS, spread, 0.0), axis=1, keepdims=True)
    weight_row = jnp.broadcast_to(weights[...], (GROUPS, GROUPS))
    here = lax.broadcasted_iota(jnp.int32, (GROUPS, GROUPS), 0) == lax.broadcasted_iota(
        jnp.int32, (GROUPS, GROUPS), 1
    )
    weight = jnp.sum(jnp.where(here, weight_row, 0.0), axis=1, keepdims=True)
    threshold = step_size * weight * jnp.sqrt(counts)
    factor = jnp.maximum(0.0, 1.0 - threshold / jnp.sqrt(squares + epsilon))
    factor = jnp.broadcast_to(factor, (GROUPS, LANES))
    for at in range(snps // LANES):
        cut = slice(at * LANES, (at + 1) * LANES)
        chosen = jnp.sum(jnp.where(ids[:, cut] == group, factor, 0.0), axis=0, keepdims=True)
        value = proposal[:, cut] * chosen
        updated[:, cut] = value
        low[:, cut] = value.astype(jnp.bfloat16)
    write_out = pltpu.make_async_copy(updated, updated_out, out_sem)
    write_out.start()
    half = rows // 2
    left = lax.broadcasted_iota(jnp.int32, (half, LANES), 1) < LANES // 2

    def per_block(step, carry):
        people = pl.ds(pl.multiple_of(step * block, block), block)
        product = lax.dot_general(low[...], dosage[people, :], NT, preferred_element_type=jnp.float32) * scale
        for at in range(block // LANES):
            cut = product[:, at * LANES : (at + 1) * LANES]
            first, second = cut[:half], cut[half:]
            index = step * (2 * block // LANES) + 2 * at
            partial[index] = jnp.where(left, first, pltpu.roll(second, LANES // 2, 1)).astype(partial.dtype)
            partial[index + 1] = jnp.where(left, pltpu.roll(first, LANES // 2, 1), second).astype(partial.dtype)
        return carry

    lax.fori_loop(0, dosage.shape[0] // block, per_block, 0)
    write_out.wait()


def score_step(sums, weights, ids, proposal, dosage, genome_count):
    rows, snps = proposal.shape
    persons = dosage.shape[0]
    vmem = pl.BlockSpec(memory_space=pltpu.VMEM)
    return pl.pallas_call(
        functools.partial(score_kernel, 1.0 / math.sqrt(snps * genome_count)),
        in_specs=[vmem] * 5,
        out_specs=[pl.BlockSpec(memory_space=pltpu.HBM), vmem],
        out_shape=[
            jax.ShapeDtypeStruct((rows, snps), jnp.float32),
            jax.ShapeDtypeStruct((genome_count, rows // 2, LANES), jnp.bfloat16),
        ],
        scratch_shapes=[
            pltpu.VMEM((rows, snps), jnp.bfloat16),
            pltpu.VMEM((rows, snps), jnp.float32),
            pltpu.SemaphoreType.DMA,
        ],
        compiler_params=pltpu.CompilerParams(vmem_limit_bytes=8 << 20),
        cost_estimate=pl.CostEstimate(
            flops=2 * rows * snps * persons, bytes_accessed=2 * snps * persons + 8 * rows * snps, transcendentals=0
        ),
        name="score_step",
    )(sums, weights, ids, proposal, dosage)


def total_kernel(arrived, scores):
    total = jnp.sum(arrived[...].astype(jnp.float32), axis=0)
    half = LANES // 2
    rows = total.shape[0]
    scores[:rows] = total[:, :half]
    scores[rows:] = pltpu.roll(total, half, 1)[:, :half]


def total_step(arrived):
    rows = 2 * arrived.shape[1]
    return pl.pallas_call(
        total_kernel,
        in_specs=[pl.BlockSpec(memory_space=pltpu.VMEM)],
        out_specs=pl.BlockSpec(memory_space=pltpu.VMEM),
        out_shape=jax.ShapeDtypeStruct((rows, LANES // 2), jnp.float32),
        name="total_step",
    )(arrived)


def swapped(block, axis, distance, lower):
    count = lax.axis_size(axis)
    pairs = [(i, i + distance) for i in range(count - distance) if lower(i)]
    return lax.ppermute(block, axis, pairs + [(j, i) for i, j in pairs])


def per_device(coefficients, sumstats, linkage, band_start, group_ids, group_weight, dosage):
    current = coefficients[0]
    targets = sumstats[0]
    band = linkage[0]
    genome_count = lax.axis_size("genome")
    anc_count = lax.axis_size("anc")
    low_copy = current.astype(jnp.bfloat16)
    near_even = swapped(low_copy, "genome", 1, lambda i: i % 2 == 0)
    near_odd = swapped(low_copy, "genome", 1, lambda i: i % 2 == 1)
    core_copy = swapped(low_copy, "anc", 1, lambda i: i % 2 == 0)
    pair_sum = (current + core_copy.astype(jnp.float32)).astype(jnp.bfloat16)
    pair_sum, own_copy = lax.optimization_barrier((pair_sum, low_copy))
    pair_copy = swapped(pair_sum, "anc", 2, lambda i: i < 2)
    own_product, early = own_step(band_start, own_copy, band, EARLY)
    near_even, near_odd, own_product = lax.optimization_barrier((near_even, near_odd, own_product))
    far_even = swapped(near_odd, "genome", 1, lambda i: i % 2 == 0)
    far_odd = swapped(near_even, "genome", 1, lambda i: i % 2 == 1)
    product, late = near_step(band_start, low_copy, near_even, near_odd, early, own_product, band)
    peers = genome_count * lax.axis_size("trait")
    proposal, sums = far_step(
        band_start, far_even, far_odd, early, late, product, current, targets, core_copy, pair_copy,
        group_ids, peers, anc_count,
    )
    arrived = lax.all_to_all(
        sums.reshape(peers, 1, LANES), ("genome", "trait"), split_axis=0, concat_axis=0, tiled=True
    ).reshape(peers, LANES)
    updated, partial = score_step(arrived, group_weight, group_ids, proposal, dosage[0], genome_count)
    received = lax.all_to_all(partial, "genome", split_axis=0, concat_axis=0, tiled=True)
    scores = total_step(received)
    return (updated[None], scores[None])


def solution(mesh):
    in_specs = (
        P("anc", "trait", "genome"),
        P("anc", "trait", "genome"),
        P("anc", "genome", None),
        P("anc", "genome"),
        P("anc", "genome"),
        P("anc", None),
        P("anc", None, "genome"),
    )
    out_specs = (P("anc", "trait", "genome"), P("anc", "trait", "genome"))
    return jax.shard_map(
        per_device, mesh=mesh, in_specs=in_specs, out_specs=out_specs, check_vma=False
    )
```

```python
import functools
import math

import jax
import jax.numpy as jnp
from jax import lax
from jax.experimental import pallas as pl
from jax.experimental.pallas import tpu as pltpu
from jax.sharding import PartitionSpec as P

TILE = 256
LANES = 128
GROUPS = 64
EARLY = 7

step_size = 0.5
merging = 0.5
epsilon = 1e-06

NT = (((1,), (1,)), ((), ()))


def place_of():
    return lax.axis_index("genome")


def window_tiles(source, base, shift, count):
    rows = source.shape[0]
    back = lax.rem(LANES - shift, LANES)
    keep = lax.broadcasted_iota(jnp.int32, (rows, LANES), 1) < LANES - shift
    tiles = []
    turned = pltpu.roll(source[:, pl.ds(base, LANES)], back, 1)
    for at in range(count):
        following = pltpu.roll(source[:, pl.ds(base + (at + 1) * LANES, LANES)], back, 1)
        tiles.append(jnp.where(keep, turned, following).astype(jnp.bfloat16))
        turned = following
    return jnp.concatenate(tiles, axis=1)


def unit_copy(band, held, sems, unit, first):
    here = pl.ds(pl.multiple_of((unit - first) * TILE, TILE), TILE)
    there = pl.ds(pl.multiple_of(unit * TILE, TILE), TILE)
    return pltpu.make_async_copy(band.at[there], held.at[here], sems.at[unit - first])


def own_kernel(starts_in, own, band, product, held, padded, starts, sems, start_sem):
    rows, snps = own.shape
    units = held.shape[0] // TILE
    count = snps // TILE + 1
    depth = min(3, units)
    start_copy = pltpu.make_async_copy(starts_in, starts, start_sem)
    start_copy.start()
    for unit in range(depth):
        unit_copy(band, held, sems, unit, 0).start()
    place = place_of()
    padded[:, :snps] = jnp.zeros((rows, snps), jnp.float32)
    padded[:, snps : 2 * snps] = own[...].astype(jnp.float32)
    padded[:, 2 * snps :] = jnp.zeros((rows, padded.shape[1] - 2 * snps), jnp.float32)
    start_copy.wait()

    def per_unit(unit, carry):
        start = starts[0, unit] + (2 - place) * snps
        first_tile = jnp.clip((2 * snps - start) // TILE, 0, snps // TILE - 1)
        column = pl.multiple_of(first_tile * TILE, TILE)
        begin = start + column - snps
        base = pl.multiple_of((begin // LANES) * LANES, LANES)
        window = window_tiles(padded, base, begin - base, count * TILE // LANES)
        cut = pl.ds(pl.multiple_of(unit * TILE, TILE), TILE)
        unit_copy(band, held, sems, unit, 0).wait()

        @pl.when(unit + depth < units)
        def _():
            unit_copy(band, held, sems, unit + depth, 0).start()

        product[:, cut] = lax.dot_general(
            window, held[cut, pl.ds(column, count * TILE)], NT, preferred_element_type=jnp.float32
        )
        return carry

    lax.fori_loop(0, units, per_unit, 0)


def own_step(starts, own, band, units):
    rows, snps = own.shape
    width = band.shape[1]
    hbm = pl.BlockSpec(memory_space=pltpu.HBM)
    vmem = pl.BlockSpec(memory_space=pltpu.VMEM)
    return pl.pallas_call(
        own_kernel,
        in_specs=[hbm, vmem, hbm],
        out_specs=[vmem, vmem],
        out_shape=[
            jax.ShapeDtypeStruct((rows, units * TILE), jnp.float32),
            jax.ShapeDtypeStruct((units * TILE, width), band.dtype),
        ],
        scratch_shapes=[
            pltpu.VMEM((rows, 3 * snps + TILE + LANES), jnp.float32),
            pltpu.SMEM((1, snps // TILE), jnp.int32),
            pltpu.SemaphoreType.DMA((units,)),
            pltpu.SemaphoreType.DMA,
        ],
        compiler_params=pltpu.CompilerParams(vmem_limit_bytes=10 << 20),
        cost_estimate=pl.CostEstimate(
            flops=2 * rows * units * TILE * (snps + TILE), bytes_accessed=2 * units * TILE * width, transcendentals=0
        ),
        name="own_step",
    )(pltpu.with_memory_space_constraint(starts, pltpu.HBM), own, pltpu.with_memory_space_constraint(band, pltpu.HBM))


def near_kernel(
    starts_in, own, first, second, early, before, band, product, late, extended, starts, sems, start_sem
):
    rows, snps = first.shape
    width = band.shape[1]
    units = snps // TILE
    early_units = early.shape[0] // TILE
    count = units + 1
    start_copy = pltpu.make_async_copy(starts_in, starts, start_sem)
    start_copy.start()
    for unit in range(early_units, units):
        unit_copy(band, late, sems, unit, early_units).start()
    place = place_of()
    first_at = jnp.where(lax.rem(place, 2) == 0, 3 * snps, snps)
    for at in (0, 2, 4):
        extended[:, at * snps : (at + 1) * snps] = jnp.zeros((rows, snps), jnp.float32)
    extended[:, 5 * snps :] = jnp.zeros((rows, LANES), jnp.float32)
    for at, piece in ((first_at, first), (4 * snps - first_at, second)):
        extended[:, pl.ds(pl.multiple_of(at, LANES), snps)] = piece[...].astype(jnp.float32)
    start_copy.wait()

    def early_unit(unit, carry):
        start = starts[0, unit] + (2 - place) * snps
        cut = pl.ds(pl.multiple_of(unit * TILE, TILE), TILE)
        left = (2 * snps - start) // TILE
        skip = jnp.where(
            start > 2 * snps, (3 * snps - start) // TILE, jnp.where(start <= snps, (snps - start) // TILE, 0)
        )
        skip = jnp.clip(skip, 0, count - 2)
        both = (start > snps) & (start <= 2 * snps)
        total = before[:, cut]
        for step in range(count):
            tile = step + jnp.where(both & (step > left), count - 2, skip)
            column = pl.multiple_of(tile * TILE, TILE)
            begin = start + column
            base = pl.multiple_of((begin // LANES) * LANES, LANES)
            window = window_tiles(extended, base, begin - base, TILE // LANES)
            total += lax.dot_general(window, early[cut, pl.ds(column, TILE)], NT, preferred_element_type=jnp.float32)
        product[:, cut] = total
        return carry

    lax.fori_loop(0, early_units, early_unit, 0)
    extended[:, 2 * snps : 3 * snps] = own[...].astype(jnp.float32)

    def late_unit(unit, carry):
        start = starts[0, unit] + (2 - place) * snps
        base = pl.multiple_of((start // LANES) * LANES, LANES)
        window = window_tiles(extended, base, start - base, width // LANES)
        unit_copy(band, late, sems, unit, early_units).wait()
        here = pl.ds(pl.multiple_of((unit - early_units) * TILE, TILE), TILE)
        cut = pl.ds(pl.multiple_of(unit * TILE, TILE), TILE)
        product[:, cut] = lax.dot_general(window, late[here, :], NT, preferred_element_type=jnp.float32)
        return carry

    lax.fori_loop(early_units, units, late_unit, 0)


def near_step(starts, own, first, second, early, before, band):
    rows, snps = first.shape
    width = band.shape[1]
    late_rows = snps - early.shape[0]
    hbm = pl.BlockSpec(memory_space=pltpu.HBM)
    vmem = pl.BlockSpec(memory_space=pltpu.VMEM)
    return pl.pallas_call(
        near_kernel,
        in_specs=[hbm] + [vmem] * 5 + [hbm],
        out_specs=[vmem, vmem],
        out_shape=[
            jax.ShapeDtypeStruct((rows, snps), jnp.float32),
            jax.ShapeDtypeStruct((late_rows, width), band.dtype),
        ],
        scratch_shapes=[
            pltpu.VMEM((rows, 5 * snps + LANES), jnp.float32),
            pltpu.SMEM((1, snps // TILE), jnp.int32),
            pltpu.SemaphoreType.DMA((late_rows // TILE,)),
            pltpu.SemaphoreType.DMA,
        ],
        compiler_params=pltpu.CompilerParams(vmem_limit_bytes=10 << 20),
        cost_estimate=pl.CostEstimate(
            flops=2 * rows * snps * width, bytes_accessed=2 * late_rows * width + 8 * rows * snps, transcendentals=0
        ),
        name="near_step",
    )(
        pltpu.with_memory_space_constraint(starts, pltpu.HBM), own, first, second, early, before,
        pltpu.with_memory_space_constraint(band, pltpu.HBM),
    )


def far_kernel(
    ancestries, starts_in, first, second, early, late, product, coef, targets, core_copy, pair_copy, ids,
    proposal, sums, far, square_acc, count_acc, bands_ref, starts, start_sem,
):
    rows, snps = coef.shape
    units = snps // TILE
    widths = (0, 2, 4, 8)
    place = place_of()
    high_at = 2 * snps + TILE
    first_at = jnp.where(lax.rem(place, 2) == 0, high_at, 0)
    start_copy = pltpu.make_async_copy(starts_in, starts, start_sem)
    start_copy.start()
    far[:, snps:high_at] = jnp.zeros((rows, high_at - snps), jnp.float32)
    far[:, high_at + snps :] = jnp.zeros((rows, LANES), jnp.float32)
    for at, piece in ((first_at, first), (high_at - first_at, second)):
        far[:, pl.ds(pl.multiple_of(at, LANES), piece.shape[1])] = piece[...].astype(jnp.float32)
    square_acc[...] = jnp.zeros_like(square_acc)
    count_acc[...] = jnp.zeros_like(count_acc)
    start_copy.wait()
    group = lax.broadcasted_iota(jnp.int32, (GROUPS, LANES), 0)

    def per_unit(held, first_unit, unit, carry):
        cut = pl.ds(pl.multiple_of(unit * TILE, TILE), TILE)
        here = pl.ds(pl.multiple_of((unit - first_unit) * TILE, TILE), TILE)
        start = starts[0, unit] + (2 - place) * snps
        tiles = held.shape[1] // TILE
        low_count = (jnp.maximum(snps - start, 0) + TILE - 1) // TILE
        high_count = (jnp.maximum(start - 2 * snps, 0) + TILE - 1) // TILE
        above = high_count > 0
        needed = low_count + high_count
        choice = sum((needed > width).astype(jnp.int32) for width in widths[:-1])
        bands_ref[...] = product[:, cut]
        for option, width in enumerate(widths):
            if width == 0:
                continue

            @pl.when(choice == option)
            def _():
                column = pl.multiple_of(jnp.where(above, tiles - width, 0) * TILE, TILE)
                begin = start + column + jnp.where(above, high_at - 4 * snps, 0)
                base = pl.multiple_of((begin // LANES) * LANES, LANES)
                window = window_tiles(far, base, begin - base, width * TILE // LANES)
                bands_ref[...] += lax.dot_general(
                    window, held[here, pl.ds(column, width * TILE)], NT, preferred_element_type=jnp.float32
                )

        bands = bands_ref[...]
        current = coef[:, cut]
        total = current + core_copy[:, cut].astype(jnp.float32) + pair_copy[:, cut].astype(jnp.float32)
        gradient = current + bands - targets[:, cut] + merging * (current - total * (1.0 / ancestries))
        value = current - step_size * gradient
        proposal[:, cut] = value
        part = jnp.sum(value * value, axis=0, keepdims=True)
        ids_here = ids[:, cut]
        squares = square_acc[...]
        counts = count_acc[...]
        for at in range(TILE // LANES):
            here = ids_here[:, at * LANES : (at + 1) * LANES] == group
            squares += jnp.where(here, part[:, at * LANES : (at + 1) * LANES], 0.0)
            counts += jnp.where(here, 1.0, 0.0)
        square_acc[...] = squares
        count_acc[...] = counts
        return carry

    early_units = early.shape[0] // TILE
    lax.fori_loop(0, early_units, functools.partial(per_unit, early, 0), 0)
    lax.fori_loop(early_units, units, functools.partial(per_unit, late, early_units), 0)
    lane = lax.broadcasted_iota(jnp.int32, (GROUPS, LANES), 1)
    square_col = jnp.sum(square_acc[...], axis=1, keepdims=True)
    count_col = jnp.sum(count_acc[...], axis=1, keepdims=True)
    both = jnp.where(lane == group, square_col, 0.0) + jnp.where(lane == group + GROUPS, count_col * rows, 0.0)
    sums[...] = jnp.broadcast_to(jnp.sum(both, axis=0, keepdims=True), sums.shape)


def far_step(starts, first, second, early, late, product, coef, targets, core_copy, pair_copy, ids, peers, ancestries):
    rows, snps = coef.shape
    hbm = pl.BlockSpec(memory_space=pltpu.HBM)
    vmem = pl.BlockSpec(memory_space=pltpu.VMEM)
    return pl.pallas_call(
        functools.partial(far_kernel, ancestries),
        in_specs=[hbm] + [vmem] * 10,
        out_specs=[vmem, vmem],
        out_shape=[
            jax.ShapeDtypeStruct((rows, snps), jnp.float32),
            jax.ShapeDtypeStruct((peers, LANES), jnp.float32),
        ],
        scratch_shapes=[
            pltpu.VMEM((rows, 3 * snps + TILE + LANES), jnp.float32),
            pltpu.VMEM((GROUPS, LANES), jnp.float32),
            pltpu.VMEM((GROUPS, LANES), jnp.float32),
            pltpu.VMEM((rows, TILE), jnp.float32),
            pltpu.SMEM((1, snps // TILE), jnp.int32),
            pltpu.SemaphoreType.DMA,
        ],
        compiler_params=pltpu.CompilerParams(vmem_limit_bytes=10 << 20),
        cost_estimate=pl.CostEstimate(
            flops=2 * rows * snps * 1024, bytes_accessed=20 * rows * snps, transcendentals=0
        ),
        name="far_step",
    )(
        pltpu.with_memory_space_constraint(starts, pltpu.HBM), first, second, early, late, product, coef, targets, core_copy, pair_copy, ids,
    )


def score_kernel(scale, sums, weights, ids, proposal, dosage, updated_out, partial, low, updated, out_sem):
    rows, snps = proposal.shape
    block = TILE
    total = jnp.sum(sums[...], axis=0, keepdims=True)
    spread = jnp.broadcast_to(total, (GROUPS, LANES))
    group = lax.broadcasted_iota(jnp.int32, (GROUPS, LANES), 0)
    place = lax.broadcasted_iota(jnp.int32, (GROUPS, LANES), 1)
    squares = jnp.sum(jnp.where(place == group, spread, 0.0), axis=1, keepdims=True)
    counts = jnp.sum(jnp.where(place == group + GROUPS, spread, 0.0), axis=1, keepdims=True)
    weight_row = jnp.broadcast_to(weights[...], (GROUPS, GROUPS))
    here = lax.broadcasted_iota(jnp.int32, (GROUPS, GROUPS), 0) == lax.broadcasted_iota(
        jnp.int32, (GROUPS, GROUPS), 1
    )
    weight = jnp.sum(jnp.where(here, weight_row, 0.0), axis=1, keepdims=True)
    threshold = step_size * weight * jnp.sqrt(counts)
    factor = jnp.maximum(0.0, 1.0 - threshold / jnp.sqrt(squares + epsilon))
    factor = jnp.broadcast_to(factor, (GROUPS, LANES))
    for at in range(snps // LANES):
        cut = slice(at * LANES, (at + 1) * LANES)
        chosen = jnp.sum(jnp.where(ids[:, cut] == group, factor, 0.0), axis=0, keepdims=True)
        value = proposal[:, cut] * chosen
        updated[:, cut] = value
        low[:, cut] = value.astype(jnp.bfloat16)
    write_out = pltpu.make_async_copy(updated, updated_out, out_sem)
    write_out.start()
    half = rows // 2
    left = lax.broadcasted_iota(jnp.int32, (half, LANES), 1) < LANES // 2

    def per_block(step, carry):
        people = pl.ds(pl.multiple_of(step * block, block), block)
        product = lax.dot_general(low[...], dosage[people, :], NT, preferred_element_type=jnp.float32) * scale
        for at in range(block // LANES):
            cut = product[:, at * LANES : (at + 1) * LANES]
            first, second = cut[:half], cut[half:]
            index = step * (2 * block // LANES) + 2 * at
            partial[index] = jnp.where(left, first, pltpu.roll(second, LANES // 2, 1)).astype(partial.dtype)
            partial[index + 1] = jnp.where(left, pltpu.roll(first, LANES // 2, 1), second).astype(partial.dtype)
        return carry

    lax.fori_loop(0, dosage.shape[0] // block, per_block, 0)
    write_out.wait()


def score_step(sums, weights, ids, proposal, dosage, genome_count):
    rows, snps = proposal.shape
    persons = dosage.shape[0]
    vmem = pl.BlockSpec(memory_space=pltpu.VMEM)
    return pl.pallas_call(
        functools.partial(score_kernel, 1.0 / math.sqrt(snps * genome_count)),
        in_specs=[vmem] * 5,
        out_specs=[pl.BlockSpec(memory_space=pltpu.HBM), vmem],
        out_shape=[
            jax.ShapeDtypeStruct((rows, snps), jnp.float32),
            jax.ShapeDtypeStruct((genome_count, rows // 2, LANES), jnp.bfloat16),
        ],
        scratch_shapes=[
            pltpu.VMEM((rows, snps), jnp.bfloat16),
            pltpu.VMEM((rows, snps), jnp.float32),
            pltpu.SemaphoreType.DMA,
        ],
        compiler_params=pltpu.CompilerParams(vmem_limit_bytes=8 << 20),
        cost_estimate=pl.CostEstimate(
            flops=2 * rows * snps * persons, bytes_accessed=2 * snps * persons + 8 * rows * snps, transcendentals=0
        ),
        name="score_step",
    )(sums, weights, ids, proposal, dosage)


def total_kernel(arrived, scores):
    total = jnp.sum(arrived[...].astype(jnp.float32), axis=0)
    half = LANES // 2
    rows = total.shape[0]
    scores[:rows] = total[:, :half]
    scores[rows:] = pltpu.roll(total, half, 1)[:, :half]


def total_step(arrived):
    rows = 2 * arrived.shape[1]
    return pl.pallas_call(
        total_kernel,
        in_specs=[pl.BlockSpec(memory_space=pltpu.VMEM)],
        out_specs=pl.BlockSpec(memory_space=pltpu.VMEM),
        out_shape=jax.ShapeDtypeStruct((rows, LANES // 2), jnp.float32),
        name="total_step",
    )(arrived)


def swapped(block, axis, distance, lower):
    count = lax.axis_size(axis)
    pairs = [(i, i + distance) for i in range(count - distance) if lower(i)]
    return lax.ppermute(block, axis, pairs + [(j, i) for i, j in pairs])


def per_device(coefficients, sumstats, linkage, band_start, group_ids, group_weight, dosage):
    current = coefficients[0]
    targets = sumstats[0]
    band = linkage[0]
    genome_count = lax.axis_size("genome")
    anc_count = lax.axis_size("anc")
    low_copy = current.astype(jnp.bfloat16)
    near_even = swapped(low_copy, "genome", 1, lambda i: i % 2 == 0)
    near_odd = swapped(low_copy, "genome", 1, lambda i: i % 2 == 1)
    core_copy = swapped(low_copy, "anc", 1, lambda i: i % 2 == 0)
    pair_sum = (current + core_copy.astype(jnp.float32)).astype(jnp.bfloat16)
    pair_sum, own_copy = lax.optimization_barrier((pair_sum, low_copy))
    pair_copy = swapped(pair_sum, "anc", 2, lambda i: i < 2)
    own_product, early = own_step(band_start, own_copy, band, EARLY)
    near_even, near_odd, own_product = lax.optimization_barrier((near_even, near_odd, own_product))
    far_even = swapped(near_odd, "genome", 1, lambda i: i % 2 == 0)
    far_odd = swapped(near_even, "genome", 1, lambda i: i % 2 == 1)
    product, late = near_step(band_start, low_copy, near_even, near_odd, early, own_product, band)
    peers = genome_count * lax.axis_size("trait")
    proposal, sums = far_step(
        band_start, far_even, far_odd, early, late, product, current, targets, core_copy, pair_copy,
        group_ids, peers, anc_count,
    )
    arrived = lax.all_to_all(
        sums.reshape(peers, 1, LANES), ("genome", "trait"), split_axis=0, concat_axis=0, tiled=True
    ).reshape(peers, LANES)
    updated, partial = score_step(arrived, group_weight, group_ids, proposal, dosage[0], genome_count)
    received = lax.all_to_all(partial, "genome", split_axis=0, concat_axis=0, tiled=True)
    scores = total_step(received)
    return (updated[None], scores[None])


def solution(mesh):
    in_specs = (
        P("anc", "trait", "genome"),
        P("anc", "trait", "genome"),
        P("anc", "genome", None),
        P("anc", "genome"),
        P("anc", "genome"),
        P("anc", None),
        P("anc", None, "genome"),
    )
    out_specs = (P("anc", "trait", "genome"), P("anc", "trait", "genome"))
    return jax.shard_map(
        per_device, mesh=mesh, in_specs=in_specs, out_specs=out_specs, check_vma=False
    )
```

```python
import functools
import math

import jax
import jax.numpy as jnp
from jax import lax
from jax.experimental import pallas as pl
from jax.experimental.pallas import tpu as pltpu
from jax.sharding import PartitionSpec as P

TILE = 256
LANES = 128
GROUPS = 64
EARLY = 7
FIRST_HALF = 4

step_size = 0.5
merging = 0.5
epsilon = 1e-06

NT = (((1,), (1,)), ((), ()))


def place_of():
    return lax.axis_index("genome")


def window_tiles(source, base, shift, count):
    rows = source.shape[0]
    back = lax.rem(LANES - shift, LANES)
    keep = lax.broadcasted_iota(jnp.int32, (rows, LANES), 1) < LANES - shift
    tiles = []
    turned = pltpu.roll(source[:, pl.ds(base, LANES)], back, 1)
    for at in range(count):
        following = pltpu.roll(source[:, pl.ds(base + (at + 1) * LANES, LANES)], back, 1)
        tiles.append(jnp.where(keep, turned, following).astype(jnp.bfloat16))
        turned = following
    return jnp.concatenate(tiles, axis=1)


def unit_copy(band, held, sems, unit, first):
    here = pl.ds(pl.multiple_of((unit - first) * TILE, TILE), TILE)
    there = pl.ds(pl.multiple_of(unit * TILE, TILE), TILE)
    return pltpu.make_async_copy(band.at[there], held.at[here], sems.at[unit - first])


def own_kernel(starts_in, own, band, product, held, padded, starts, sems, start_sem):
    rows, snps = own.shape
    units = held.shape[0] // TILE
    count = snps // TILE + 1
    depth = min(3, units)
    start_copy = pltpu.make_async_copy(starts_in, starts, start_sem)
    start_copy.start()
    for unit in range(depth):
        unit_copy(band, held, sems, unit, 0).start()
    place = place_of()
    padded[:, :snps] = jnp.zeros((rows, snps), jnp.float32)
    padded[:, snps : 2 * snps] = own[...].astype(jnp.float32)
    padded[:, 2 * snps :] = jnp.zeros((rows, padded.shape[1] - 2 * snps), jnp.float32)
    start_copy.wait()

    def per_unit(unit, carry):
        start = starts[0, unit] + (2 - place) * snps
        first_tile = jnp.clip((2 * snps - start) // TILE, 0, snps // TILE - 1)
        column = pl.multiple_of(first_tile * TILE, TILE)
        begin = start + column - snps
        base = pl.multiple_of((begin // LANES) * LANES, LANES)
        window = window_tiles(padded, base, begin - base, count * TILE // LANES)
        cut = pl.ds(pl.multiple_of(unit * TILE, TILE), TILE)
        unit_copy(band, held, sems, unit, 0).wait()

        @pl.when(unit + depth < units)
        def _():
            unit_copy(band, held, sems, unit + depth, 0).start()

        product[:, cut] = lax.dot_general(
            window, held[cut, pl.ds(column, count * TILE)], NT, preferred_element_type=jnp.float32
        )
        return carry

    lax.fori_loop(0, units, per_unit, 0)


def own_step(starts, own, band, units):
    rows, snps = own.shape
    width = band.shape[1]
    hbm = pl.BlockSpec(memory_space=pltpu.HBM)
    vmem = pl.BlockSpec(memory_space=pltpu.VMEM)
    return pl.pallas_call(
        own_kernel,
        in_specs=[hbm, vmem, hbm],
        out_specs=[vmem, vmem],
        out_shape=[
            jax.ShapeDtypeStruct((rows, units * TILE), jnp.float32),
            jax.ShapeDtypeStruct((units * TILE, width), band.dtype),
        ],
        scratch_shapes=[
            pltpu.VMEM((rows, 3 * snps + TILE + LANES), jnp.float32),
            pltpu.SMEM((1, snps // TILE), jnp.int32),
            pltpu.SemaphoreType.DMA((units,)),
            pltpu.SemaphoreType.DMA,
        ],
        compiler_params=pltpu.CompilerParams(vmem_limit_bytes=10 << 20),
        cost_estimate=pl.CostEstimate(
            flops=2 * rows * units * TILE * (snps + TILE), bytes_accessed=2 * units * TILE * width, transcendentals=0
        ),
        name="own_step",
    )(pltpu.with_memory_space_constraint(starts, pltpu.HBM), own, pltpu.with_memory_space_constraint(band, pltpu.HBM))


def half_kernel(from_unit, to_unit, starts_in, first, second, early, before, product, extended, starts, start_sem):
    near_body(
        from_unit, to_unit, starts_in, None, first, second, early, before, None, product, None, extended, starts,
        None, start_sem,
    )


def rest_kernel(
    from_unit, starts_in, own, first, second, early, before, band, product, late, extended, starts, sems, start_sem
):
    near_body(
        from_unit, first.shape[1] // TILE, starts_in, own, first, second, early, before, band, product, late,
        extended, starts, sems, start_sem,
    )


def near_body(
    from_unit, to_unit, starts_in, own, first, second, early, before, band, product, late, extended, starts, sems,
    start_sem,
):
    rows, snps = first.shape
    width = early.shape[1]
    early_units = min(early.shape[0] // TILE, to_unit)
    count = snps // TILE + 1
    start_copy = pltpu.make_async_copy(starts_in, starts, start_sem)
    start_copy.start()
    for unit in range(early_units, to_unit):
        unit_copy(band, late, sems, unit, early_units).start()
    place = place_of()
    first_at = jnp.where(lax.rem(place, 2) == 0, 3 * snps, snps)
    for at in (0, 2, 4):
        extended[:, at * snps : (at + 1) * snps] = jnp.zeros((rows, snps), jnp.float32)
    extended[:, 5 * snps :] = jnp.zeros((rows, LANES), jnp.float32)
    for at, piece in ((first_at, first), (4 * snps - first_at, second)):
        extended[:, pl.ds(pl.multiple_of(at, LANES), snps)] = piece[...].astype(jnp.float32)
    start_copy.wait()

    def early_unit(unit, carry):
        start = starts[0, unit] + (2 - place) * snps
        cut = pl.ds(pl.multiple_of(unit * TILE, TILE), TILE)
        left = (2 * snps - start) // TILE
        skip = jnp.where(
            start > 2 * snps, (3 * snps - start) // TILE, jnp.where(start <= snps, (snps - start) // TILE, 0)
        )
        skip = jnp.clip(skip, 0, count - 2)
        both = (start > snps) & (start <= 2 * snps)
        total = before[:, cut]
        for step in range(count):
            tile = step + jnp.where(both & (step > left), count - 2, skip)
            column = pl.multiple_of(tile * TILE, TILE)
            begin = start + column
            base = pl.multiple_of((begin // LANES) * LANES, LANES)
            window = window_tiles(extended, base, begin - base, TILE // LANES)
            total += lax.dot_general(window, early[cut, pl.ds(column, TILE)], NT, preferred_element_type=jnp.float32)
        product[:, pl.ds(pl.multiple_of((unit - from_unit) * TILE, TILE), TILE)] = total
        return carry

    lax.fori_loop(from_unit, early_units, early_unit, 0)
    if own is None:
        return
    extended[:, 2 * snps : 3 * snps] = own[...].astype(jnp.float32)

    def late_unit(unit, carry):
        start = starts[0, unit] + (2 - place) * snps
        base = pl.multiple_of((start // LANES) * LANES, LANES)
        window = window_tiles(extended, base, start - base, width // LANES)
        unit_copy(band, late, sems, unit, early_units).wait()
        here = pl.ds(pl.multiple_of((unit - early_units) * TILE, TILE), TILE)
        cut = pl.ds(pl.multiple_of((unit - from_unit) * TILE, TILE), TILE)
        product[:, cut] = lax.dot_general(window, late[here, :], NT, preferred_element_type=jnp.float32)
        return carry

    lax.fori_loop(early_units, to_unit, late_unit, 0)


def half_step(starts, first, second, early, before, to_unit):
    rows, snps = first.shape
    hbm = pl.BlockSpec(memory_space=pltpu.HBM)
    vmem = pl.BlockSpec(memory_space=pltpu.VMEM)
    return pl.pallas_call(
        functools.partial(half_kernel, 0, to_unit),
        in_specs=[hbm] + [vmem] * 4,
        out_specs=vmem,
        out_shape=jax.ShapeDtypeStruct((rows, to_unit * TILE), jnp.float32),
        scratch_shapes=[
            pltpu.VMEM((rows, 5 * snps + LANES), jnp.float32),
            pltpu.SMEM((1, snps // TILE), jnp.int32),
            pltpu.SemaphoreType.DMA,
        ],
        compiler_params=pltpu.CompilerParams(vmem_limit_bytes=10 << 20),
        cost_estimate=pl.CostEstimate(
            flops=2 * rows * to_unit * TILE * (snps + TILE), bytes_accessed=8 * rows * snps, transcendentals=0
        ),
        name="half_step",
    )(pltpu.with_memory_space_constraint(starts, pltpu.HBM), first, second, early, before)


def near_step(starts, own, first, second, early, before, band, from_unit):
    rows, snps = first.shape
    width = band.shape[1]
    late_rows = snps - early.shape[0]
    hbm = pl.BlockSpec(memory_space=pltpu.HBM)
    vmem = pl.BlockSpec(memory_space=pltpu.VMEM)
    return pl.pallas_call(
        functools.partial(rest_kernel, from_unit),
        in_specs=[hbm] + [vmem] * 5 + [hbm],
        out_specs=[vmem, vmem],
        out_shape=[
            jax.ShapeDtypeStruct((rows, snps - from_unit * TILE), jnp.float32),
            jax.ShapeDtypeStruct((late_rows, width), band.dtype),
        ],
        scratch_shapes=[
            pltpu.VMEM((rows, 5 * snps + LANES), jnp.float32),
            pltpu.SMEM((1, snps // TILE), jnp.int32),
            pltpu.SemaphoreType.DMA((late_rows // TILE,)),
            pltpu.SemaphoreType.DMA,
        ],
        compiler_params=pltpu.CompilerParams(vmem_limit_bytes=10 << 20),
        cost_estimate=pl.CostEstimate(
            flops=2 * rows * snps * width, bytes_accessed=2 * late_rows * width + 8 * rows * snps, transcendentals=0
        ),
        name="near_step",
    )(
        pltpu.with_memory_space_constraint(starts, pltpu.HBM), own, first, second, early, before,
        pltpu.with_memory_space_constraint(band, pltpu.HBM),
    )


def far_kernel(
    ancestries, starts_in, first, second, early, late, product, rest, coef, targets, core_copy, pair_copy, ids,
    proposal, sums, far, square_acc, count_acc, bands_ref, starts, start_sem,
):
    rows, snps = coef.shape
    units = snps // TILE
    widths = (0, 2, 4, 8)
    place = place_of()
    high_at = 2 * snps + TILE
    first_at = jnp.where(lax.rem(place, 2) == 0, high_at, 0)
    start_copy = pltpu.make_async_copy(starts_in, starts, start_sem)
    start_copy.start()
    far[:, snps:high_at] = jnp.zeros((rows, high_at - snps), jnp.float32)
    far[:, high_at + snps :] = jnp.zeros((rows, LANES), jnp.float32)
    for at, piece in ((first_at, first), (high_at - first_at, second)):
        far[:, pl.ds(pl.multiple_of(at, LANES), piece.shape[1])] = piece[...].astype(jnp.float32)
    square_acc[...] = jnp.zeros_like(square_acc)
    count_acc[...] = jnp.zeros_like(count_acc)
    start_copy.wait()
    group = lax.broadcasted_iota(jnp.int32, (GROUPS, LANES), 0)

    def per_unit(held, first_unit, before, before_unit, unit, carry):
        cut = pl.ds(pl.multiple_of(unit * TILE, TILE), TILE)
        here = pl.ds(pl.multiple_of((unit - first_unit) * TILE, TILE), TILE)
        start = starts[0, unit] + (2 - place) * snps
        tiles = held.shape[1] // TILE
        low_count = (jnp.maximum(snps - start, 0) + TILE - 1) // TILE
        high_count = (jnp.maximum(start - 2 * snps, 0) + TILE - 1) // TILE
        above = high_count > 0
        needed = low_count + high_count
        choice = sum((needed > width).astype(jnp.int32) for width in widths[:-1])
        bands_ref[...] = before[:, pl.ds(pl.multiple_of((unit - before_unit) * TILE, TILE), TILE)]
        for option, width in enumerate(widths):
            if width == 0:
                continue

            @pl.when(choice == option)
            def _():
                column = pl.multiple_of(jnp.where(above, tiles - width, 0) * TILE, TILE)
                begin = start + column + jnp.where(above, high_at - 4 * snps, 0)
                base = pl.multiple_of((begin // LANES) * LANES, LANES)
                window = window_tiles(far, base, begin - base, width * TILE // LANES)
                bands_ref[...] += lax.dot_general(
                    window, held[here, pl.ds(column, width * TILE)], NT, preferred_element_type=jnp.float32
                )

        bands = bands_ref[...]
        current = coef[:, cut]
        total = current + core_copy[:, cut].astype(jnp.float32) + pair_copy[:, cut].astype(jnp.float32)
        gradient = current + bands - targets[:, cut] + merging * (current - total * (1.0 / ancestries))
        value = current - step_size * gradient
        proposal[:, cut] = value
        part = jnp.sum(value * value, axis=0, keepdims=True)
        ids_here = ids[:, cut]
        squares = square_acc[...]
        counts = count_acc[...]
        for at in range(TILE // LANES):
            here = ids_here[:, at * LANES : (at + 1) * LANES] == group
            squares += jnp.where(here, part[:, at * LANES : (at + 1) * LANES], 0.0)
            counts += jnp.where(here, 1.0, 0.0)
        square_acc[...] = squares
        count_acc[...] = counts
        return carry

    early_units = early.shape[0] // TILE
    half_units = product.shape[1] // TILE
    lax.fori_loop(0, half_units, functools.partial(per_unit, early, 0, product, 0), 0)
    lax.fori_loop(half_units, early_units, functools.partial(per_unit, early, 0, rest, half_units), 0)
    lax.fori_loop(early_units, units, functools.partial(per_unit, late, early_units, rest, half_units), 0)
    lane = lax.broadcasted_iota(jnp.int32, (GROUPS, LANES), 1)
    square_col = jnp.sum(square_acc[...], axis=1, keepdims=True)
    count_col = jnp.sum(count_acc[...], axis=1, keepdims=True)
    both = jnp.where(lane == group, square_col, 0.0) + jnp.where(lane == group + GROUPS, count_col * rows, 0.0)
    sums[...] = jnp.broadcast_to(jnp.sum(both, axis=0, keepdims=True), sums.shape)


def far_step(starts, first, second, early, late, product, rest, coef, targets, core_copy, pair_copy, ids, peers, ancestries):
    rows, snps = coef.shape
    hbm = pl.BlockSpec(memory_space=pltpu.HBM)
    vmem = pl.BlockSpec(memory_space=pltpu.VMEM)
    return pl.pallas_call(
        functools.partial(far_kernel, ancestries),
        in_specs=[hbm] + [vmem] * 11,
        out_specs=[vmem, vmem],
        out_shape=[
            jax.ShapeDtypeStruct((rows, snps), jnp.float32),
            jax.ShapeDtypeStruct((peers, LANES), jnp.float32),
        ],
        scratch_shapes=[
            pltpu.VMEM((rows, 3 * snps + TILE + LANES), jnp.float32),
            pltpu.VMEM((GROUPS, LANES), jnp.float32),
            pltpu.VMEM((GROUPS, LANES), jnp.float32),
            pltpu.VMEM((rows, TILE), jnp.float32),
            pltpu.SMEM((1, snps // TILE), jnp.int32),
            pltpu.SemaphoreType.DMA,
        ],
        compiler_params=pltpu.CompilerParams(vmem_limit_bytes=10 << 20),
        cost_estimate=pl.CostEstimate(
            flops=2 * rows * snps * 1024, bytes_accessed=20 * rows * snps, transcendentals=0
        ),
        name="far_step",
    )(
        pltpu.with_memory_space_constraint(starts, pltpu.HBM), first, second, early, late, product, rest, coef, targets, core_copy, pair_copy, ids,
    )


def score_kernel(scale, sums, weights, ids, proposal, dosage, updated_out, partial, low, updated, out_sem):
    rows, snps = proposal.shape
    block = TILE
    total = jnp.sum(sums[...], axis=0, keepdims=True)
    spread = jnp.broadcast_to(total, (GROUPS, LANES))
    group = lax.broadcasted_iota(jnp.int32, (GROUPS, LANES), 0)
    place = lax.broadcasted_iota(jnp.int32, (GROUPS, LANES), 1)
    squares = jnp.sum(jnp.where(place == group, spread, 0.0), axis=1, keepdims=True)
    counts = jnp.sum(jnp.where(place == group + GROUPS, spread, 0.0), axis=1, keepdims=True)
    weight_row = jnp.broadcast_to(weights[...], (GROUPS, GROUPS))
    here = lax.broadcasted_iota(jnp.int32, (GROUPS, GROUPS), 0) == lax.broadcasted_iota(
        jnp.int32, (GROUPS, GROUPS), 1
    )
    weight = jnp.sum(jnp.where(here, weight_row, 0.0), axis=1, keepdims=True)
    threshold = step_size * weight * jnp.sqrt(counts)
    factor = jnp.maximum(0.0, 1.0 - threshold / jnp.sqrt(squares + epsilon))
    factor = jnp.broadcast_to(factor, (GROUPS, LANES))
    for at in range(snps // LANES):
        cut = slice(at * LANES, (at + 1) * LANES)
        chosen = jnp.sum(jnp.where(ids[:, cut] == group, factor, 0.0), axis=0, keepdims=True)
        value = proposal[:, cut] * chosen
        updated[:, cut] = value
        low[:, cut] = value.astype(jnp.bfloat16)
    write_out = pltpu.make_async_copy(updated, updated_out, out_sem)
    write_out.start()
    half = rows // 2
    left = lax.broadcasted_iota(jnp.int32, (half, LANES), 1) < LANES // 2

    def per_block(step, carry):
        people = pl.ds(pl.multiple_of(step * block, block), block)
        product = lax.dot_general(low[...], dosage[people, :], NT, preferred_element_type=jnp.float32) * scale
        for at in range(block // LANES):
            cut = product[:, at * LANES : (at + 1) * LANES]
            first, second = cut[:half], cut[half:]
            index = step * (2 * block // LANES) + 2 * at
            partial[index] = jnp.where(left, first, pltpu.roll(second, LANES // 2, 1)).astype(partial.dtype)
            partial[index + 1] = jnp.where(left, pltpu.roll(first, LANES // 2, 1), second).astype(partial.dtype)
        return carry

    lax.fori_loop(0, dosage.shape[0] // block, per_block, 0)
    write_out.wait()


def score_step(sums, weights, ids, proposal, dosage, genome_count):
    rows, snps = proposal.shape
    persons = dosage.shape[0]
    vmem = pl.BlockSpec(memory_space=pltpu.VMEM)
    return pl.pallas_call(
        functools.partial(score_kernel, 1.0 / math.sqrt(snps * genome_count)),
        in_specs=[vmem] * 5,
        out_specs=[pl.BlockSpec(memory_space=pltpu.HBM), vmem],
        out_shape=[
            jax.ShapeDtypeStruct((rows, snps), jnp.float32),
            jax.ShapeDtypeStruct((genome_count, rows // 2, LANES), jnp.bfloat16),
        ],
        scratch_shapes=[
            pltpu.VMEM((rows, snps), jnp.bfloat16),
            pltpu.VMEM((rows, snps), jnp.float32),
            pltpu.SemaphoreType.DMA,
        ],
        compiler_params=pltpu.CompilerParams(vmem_limit_bytes=8 << 20),
        cost_estimate=pl.CostEstimate(
            flops=2 * rows * snps * persons, bytes_accessed=2 * snps * persons + 8 * rows * snps, transcendentals=0
        ),
        name="score_step",
    )(sums, weights, ids, proposal, dosage)


def total_kernel(arrived, scores):
    total = jnp.sum(arrived[...].astype(jnp.float32), axis=0)
    half = LANES // 2
    rows = total.shape[0]
    scores[:rows] = total[:, :half]
    scores[rows:] = pltpu.roll(total, half, 1)[:, :half]


def total_step(arrived):
    rows = 2 * arrived.shape[1]
    return pl.pallas_call(
        total_kernel,
        in_specs=[pl.BlockSpec(memory_space=pltpu.VMEM)],
        out_specs=pl.BlockSpec(memory_space=pltpu.VMEM),
        out_shape=jax.ShapeDtypeStruct((rows, LANES // 2), jnp.float32),
        name="total_step",
    )(arrived)


def swapped(block, axis, distance, lower):
    count = lax.axis_size(axis)
    pairs = [(i, i + distance) for i in range(count - distance) if lower(i)]
    return lax.ppermute(block, axis, pairs + [(j, i) for i, j in pairs])


def per_device(coefficients, sumstats, linkage, band_start, group_ids, group_weight, dosage):
    current = coefficients[0]
    targets = sumstats[0]
    band = linkage[0]
    genome_count = lax.axis_size("genome")
    anc_count = lax.axis_size("anc")
    low_copy = current.astype(jnp.bfloat16)
    near_even = swapped(low_copy, "genome", 1, lambda i: i % 2 == 0)
    near_odd = swapped(low_copy, "genome", 1, lambda i: i % 2 == 1)
    core_copy = swapped(low_copy, "anc", 1, lambda i: i % 2 == 0)
    pair_sum = (current + core_copy.astype(jnp.float32)).astype(jnp.bfloat16)
    pair_sum, own_copy = lax.optimization_barrier((pair_sum, low_copy))
    pair_copy = swapped(pair_sum, "anc", 2, lambda i: i < 2)
    own_product, early = own_step(band_start, own_copy, band, EARLY)
    near_even, near_odd, own_product = lax.optimization_barrier((near_even, near_odd, own_product))
    far_even = swapped(near_odd, "genome", 1, lambda i: i % 2 == 0)
    product = half_step(band_start, near_even, near_odd, early, own_product, FIRST_HALF)
    near_even, near_odd, product = lax.optimization_barrier((near_even, near_odd, product))
    far_odd = swapped(near_even, "genome", 1, lambda i: i % 2 == 1)
    rest, late = near_step(band_start, low_copy, near_even, near_odd, early, own_product, band, FIRST_HALF)
    peers = genome_count * lax.axis_size("trait")
    proposal, sums = far_step(
        band_start, far_even, far_odd, early, late, product, rest, current, targets, core_copy, pair_copy,
        group_ids, peers, anc_count,
    )
    arrived = lax.all_to_all(
        sums.reshape(peers, 1, LANES), ("genome", "trait"), split_axis=0, concat_axis=0, tiled=True
    ).reshape(peers, LANES)
    updated, partial = score_step(arrived, group_weight, group_ids, proposal, dosage[0], genome_count)
    received = lax.all_to_all(partial, "genome", split_axis=0, concat_axis=0, tiled=True)
    scores = total_step(received)
    return (updated[None], scores[None])


def solution(mesh):
    in_specs = (
        P("anc", "trait", "genome"),
        P("anc", "trait", "genome"),
        P("anc", "genome", None),
        P("anc", "genome"),
        P("anc", "genome"),
        P("anc", None),
        P("anc", None, "genome"),
    )
    out_specs = (P("anc", "trait", "genome"), P("anc", "trait", "genome"))
    return jax.shard_map(
        per_device, mesh=mesh, in_specs=in_specs, out_specs=out_specs, check_vma=False
    )
```
